256 devices in a mesh: blk: 8 (over y_lo, x), head: 32 (over z, y_hi, core).
Axes of the slice: x: 4, y: 4 (y_hi: 2, y_lo: 2; y = y_hi * 2 + y_lo), z: 8, core: 2. Of those that a mesh axis runs over, the one named last changes fastest.
Arguments:
- queries: bfloat16 [32768, 2048], P(('blk', 'head')), may hold values from -11 to 11
- keys: bfloat16 [32768, 2048], P(('blk', 'head')), may hold values from -11 to 11
- values: bfloat16 [32768, 2048], P(('blk', 'head')), may hold values from -6 to 6
- slopes: float32 [32], replicated, may hold values from 0.25 to 2
- layer: int32 [256], replicated, may hold values from 0 to 3, as said below
- mask: int32 [256, 256], replicated, may hold values from 0 to 1, as said below
- perm: int32 [256], replicated, may hold values from 0 to 255, as said below
Outputs:
- attended: bfloat16 [32768, 2048], P(('blk', 'head'))
The draws below stay inside these ranges and needn't reach their ends.
Inputs may be any that keep to these rules, and one draw needn't show every extreme that they name: Block c means slots c * 32 to (c + 1) * 32 - 1; a tile is active if its layer is 3. Each tile may attend to itself. mask[perm[p], perm[q]] is 0 unless the block of q is the block of p or the one before or after it, the last and the first block counting as neighbours. In each of these three blocks a tile may attend to at least one tile, to at most 9 if it is active and to at most 3 otherwise; both bounds are reached. `layer`: every block holds at most 16 slots whose tile is active, and some block holds exactly 16. `perm`: A permutation of the tiles.
All inputs are finite; a program needn't handle non-finite values.
Results may differ from the reference program's by a relative error of at most 0.0065.
Values may be sent and summed in bfloat16 or wider, within the bound.
No kernel may reach another device: no remote copies, remote signals or barrier semaphores. Data moves between devices by JAX's collectives and lax.ppermute only.
A program may use at most 64 MiB of HBM per device.

```python
import math
import jax
import jax.numpy as jnp
from jax import lax

HD = 64
HEADS = 32
D = 2048
TILE = 128
TB = 32
TOKENS = 32768
TILES = 256
NB_MOST = 3
KCAP = 9
ACT_MOST = 16
NL = 4


def layout_draw(key):
    blocks_count = TILES // TB
    blocks = jnp.arange(blocks_count, dtype=jnp.int32)
    local = jnp.arange(TB, dtype=jnp.int32)
    slots = jnp.arange(TILES, dtype=jnp.int32)
    perm = jax.random.permutation(jax.random.fold_in(key, 1), TILES).astype(jnp.int32)
    hottest = jax.random.randint(jax.random.fold_in(key, 2), (), 0, blocks_count)
    active_count = jax.random.randint(jax.random.fold_in(key, 3), (blocks_count,), 0, 2)
    active_count = jnp.where(blocks == hottest, ACT_MOST, active_count)
    picking = jax.random.randint(jax.random.fold_in(key, 4), (blocks_count, TB), 0, 2 ** 20) * TB + local[None, :]
    place_rank = jnp.argsort(jnp.argsort(picking, axis=1), axis=1)
    active = (place_rank < active_count[:, None]).reshape(TILES)
    other_layer = jax.random.randint(jax.random.fold_in(key, 5), (TILES,), 0, NL - 1)
    slot_layer = jnp.where(active, NL - 1, other_layer).astype(jnp.int32)
    amount = jax.random.randint(jax.random.fold_in(key, 6), (TILES, 3), 1, NB_MOST + 1)
    amount = jnp.where(active[:, None], 3 * amount, amount)
    hot_row = active.reshape(blocks_count, TB)[hottest].astype(jnp.int32)
    first_active = hottest * TB + jnp.argmax(hot_row)
    first_drawn = hottest * TB + jnp.argmax(1 - hot_row)
    own_amount = amount[:, 1]
    own_amount = jnp.where(slots == first_active, KCAP, own_amount)
    own_amount = jnp.where(slots == first_drawn, NB_MOST, own_amount)
    amount = amount.at[:, 1].set(own_amount)
    position = slots % TB
    choosing = jax.random.randint(jax.random.fold_in(key, 7), (TILES, 3, TB), 1, 2 ** 20) * TB + local[None, None, :]
    own_choosing = jnp.where(local[None, :] == position[:, None], 0, choosing[:, 1, :])
    choosing = choosing.at[:, 1, :].set(own_choosing)
    chosen_rank = jnp.argsort(jnp.argsort(choosing, axis=2), axis=2)
    chosen = (chosen_rank < amount[:, :, None]).astype(jnp.int32)
    target = (slots[:, None] // TB + jnp.arange(3, dtype=jnp.int32)[None, :] - 1) % blocks_count
    onehot = (target[:, :, None] == blocks[None, None, :]).astype(jnp.int32)
    slot_mask = jnp.sum(onehot[:, :, :, None] * chosen[:, :, None, :], axis=1).reshape(TILES, TILES)
    inverse = jnp.zeros((TILES,), jnp.int32).at[perm].set(slots)
    tile_mask = jnp.take(jnp.take(slot_mask, inverse, axis=0), inverse, axis=1)
    tile_layer = jnp.take(slot_layer, inverse)
    return (perm, tile_layer.astype(jnp.int32), tile_mask.astype(jnp.int32))


def draw_perm(key, part):
    return layout_draw(key)[0]


def draw_layer(key, part):
    return layout_draw(key)[1]


def draw_mask(key, part):
    return layout_draw(key)[2]


def draw_queries(key, part):
    result = jnp.clip(jax.random.normal(jax.random.fold_in(key, 31), (TOKENS, D), jnp.float32), -6.0, 6.0)
    return result.astype(jnp.bfloat16)


def draw_keys(key, part):
    result = jnp.clip(jax.random.normal(jax.random.fold_in(key, 32), (TOKENS, D), jnp.float32), -6.0, 6.0)
    return result.astype(jnp.bfloat16)


def steps_of(rng, shape, shards, smallest, top_value):
    loudness = 1.0
    for dim, parts in shards:
        heights = jax.random.uniform(jax.random.fold_in(jax.random.fold_in(rng, 6), dim), (parts,), jnp.float32, smallest / len(shards), top_value / len(shards))
        loudness = loudness * jnp.repeat(jnp.exp(heights), shape[dim] // parts).reshape((-1,) + (1,) * (len(shape) - 1 - dim))
    return loudness


def bell_draw(stream_key, dims, spread, reach, shards=(), kind=jnp.bfloat16):
    values = jax.random.normal(stream_key, dims, jnp.float32) * spread
    if len(shards) > 0:
        values = steps_of(stream_key, dims, shards, -0.22, 0.18) * values
    return jnp.clip(values, min=-reach, max=reach).astype(kind)


def setup_inputs(seed: int = 0) -> dict:
    key_list = jax.random.split(jax.random.key(seed), 8)
    return {
        "queries": draw_queries(jax.random.fold_in(key_list[7], 71), 0),
        "keys": draw_keys(jax.random.fold_in(key_list[7], 71), 0),
        "values": bell_draw(key_list[2], (TOKENS, D), 1.0, 6.0, ((0, 256),)),
        "slopes": jnp.clip(jnp.exp(jax.random.uniform(key_list[3], (HEADS,), jnp.float32, math.log(0.25), math.log(2.0))), 0.25, 2.0),
        "layer": draw_layer(jax.random.fold_in(key_list[7], 71), 0),
        "mask": draw_mask(jax.random.fold_in(key_list[7], 71), 0),
        "perm": draw_perm(jax.random.fold_in(key_list[7], 71), 0),
    }


def reference(queries, keys, values, slopes, layer, mask, perm):
    slot_layer = jnp.take(layer, perm)
    allowed = jnp.take(jnp.take(mask, perm, axis=0), perm, axis=1)
    widest = 3 * KCAP
    columns = jnp.arange(TILES, dtype=jnp.int32)
    ranking = allowed * (2 * TILES) + (TILES - columns)[None, :]
    _, partner = lax.top_k(ranking, widest)
    present = jnp.take_along_axis(allowed, partner, axis=1) == 1
    layer_gap = jnp.abs(slot_layer[:, None] - jnp.take(slot_layer, partner)).astype(jnp.float32)
    query_tiles = queries.reshape(TILES, TILE, HEADS, HD)
    key_tiles = keys.reshape(TILES, TILE, HEADS, HD)
    value_tiles = values.reshape(TILES, TILE, HEADS, HD)

    def one_tile(index):
        query_part = query_tiles[index].astype(jnp.float32)
        key_part = jnp.take(key_tiles, partner[index], axis=0).astype(jnp.float32)
        value_part = jnp.take(value_tiles, partner[index], axis=0).astype(jnp.float32)
        scores = jnp.einsum('rhc,nkhc->rhnk', query_part, key_part) / math.sqrt(HD)
        scores = scores - slopes[None, :, None, None] * layer_gap[index][None, None, :, None]
        usable = present[index][None, None, :, None]
        top_score = lax.optimization_barrier(jnp.max(jnp.where(usable, scores, -jnp.inf), axis=(2, 3)))
        weights = jnp.where(usable, jnp.exp(scores - top_score[:, :, None, None]), 0.0)
        total_weight = lax.optimization_barrier(jnp.sum(weights, axis=(2, 3)))
        rounded = lax.optimization_barrier(weights.astype(jnp.bfloat16)).astype(jnp.float32)
        mixed = jnp.einsum('rhnk,nkhc->rhc', rounded, value_part)
        return (mixed / total_weight[:, :, None]).astype(jnp.bfloat16).reshape(TILE, HEADS * HD)
    return lax.map(one_tile, jnp.arange(TILES, dtype=jnp.int32)).reshape(TOKENS, HEADS * HD)
```

```python
import math

import jax
import jax.numpy as jnp
from jax import lax
from jax.experimental import pallas as pl
from jax.experimental.pallas import tpu as pltpu
from jax.sharding import PartitionSpec as P

HD = 64
HEADS = 32
TILE = 128
TB = 32
TILES = 256
KCAP = 9
GROUP = 3
MOST_STEPS = 256
LOWEST = -1e30
EXPONENT = math.log2(math.e)

f32 = jnp.float32
bf16 = jnp.bfloat16
i32 = jnp.int32


def from_behind(value, axis, steps):
    count = lax.axis_size(axis)
    pairs = [(source, (source + steps) % count) for source in range(count)]
    return lax.ppermute(value, axis, pairs)


def pack_kv_kernel(k_ref, v_ref, kv_ref):
    for pair in range(HEADS // 2):
        columns = slice(pair * 128, pair * 128 + 128)
        k = k_ref[:, columns]
        upper, lower = k[:64], k[64:]
        kv_ref[2 * pair, :64, :] = jnp.concatenate([upper[:, :64], lower[:, :64]], axis=1)
        kv_ref[2 * pair + 1, :64, :] = jnp.concatenate([upper[:, 64:], lower[:, 64:]], axis=1)
        v = v_ref[:, columns].T
        kv_ref[2 * pair, 64:, :] = v[:64]
        kv_ref[2 * pair + 1, 64:, :] = v[64:]


def pack_kv(keys, values):
    return pl.pallas_call(
        pack_kv_kernel,
        out_shape=jax.ShapeDtypeStruct((HEADS, 128, 128), bf16),
        name="pack_kv",
    )(keys, values)


def pack_q_kernel(q_ref, out_ref):
    for pair in range(HEADS // 2):
        q = q_ref[:, pair * 128 : pair * 128 + 128].T
        out_ref[2 * pair] = q[:64]
        out_ref[2 * pair + 1] = q[64:]


def pack_q(queries):
    return pl.pallas_call(
        pack_q_kernel,
        out_shape=jax.ShapeDtypeStruct((HEADS, HD, 128), bf16),
        name="pack_q",
    )(queries)


def unpack_kernel(in_ref, out_ref):
    for pair in range(HEADS // 2):
        both = jnp.concatenate([in_ref[2 * pair], in_ref[2 * pair + 1]], axis=0)
        out_ref[:, pair * 128 : pair * 128 + 128] = both.T


def unpack(array):
    return pl.pallas_call(
        unpack_kernel,
        out_shape=jax.ShapeDtypeStruct((128, HEADS * HD), bf16),
        name="unpack",
    )(array)


def iota(shape, dim):
    return lax.broadcasted_iota(i32, shape, dim)


def exact_dot(a, b):
    return jnp.dot(a.astype(bf16), b.astype(bf16), preferred_element_type=f32)


def table_kernel(block_ref, perm_ref, layer_ref, mask_ref, out_ref):
    block = block_ref[0]
    shift = lax.rem(TILES + TB - block * TB, TILES)
    perm = pltpu.roll(jnp.broadcast_to(perm_ref[...], (8, TILES)), shift, 1)[:1, :128]
    select = (perm == iota((TILES, 128), 0)).astype(f32)
    select_t = select.T
    own_select = select_t[TB : 2 * TB]
    columns = exact_dot(mask_ref[...].astype(f32), select)
    allowed = exact_dot(own_select, columns)
    allowed = jnp.where(iota((TB, 128), 1) < 3 * TB, allowed, 0.0)
    layer = layer_ref[...].astype(f32)
    layer_row = exact_dot(jnp.broadcast_to(layer, (8, TILES)), select)[:1]
    layer_own = jnp.sum(own_select * layer, axis=1, keepdims=True)
    gap = jnp.abs(layer_own - layer_row)
    before = (iota((128, 128), 0) < iota((128, 128), 1)).astype(f32)
    place = exact_dot(allowed, before)
    place = jnp.where(allowed > 0.5, place, 200.0)
    count = jnp.sum(allowed, axis=1, keepdims=True)
    steps = jnp.zeros((TB, 1), f32)
    for filled in range(0, 3 * KCAP, GROUP):
        steps = steps + (count > filled + 0.5).astype(f32)
    steps = jnp.broadcast_to(steps, (TB, 128))
    earlier = (iota((TB, TB), 1) < iota((TB, TB), 0)).astype(f32)
    start = exact_dot(earlier, steps)
    start = jnp.concatenate([start, start], axis=1)
    steps = jnp.concatenate([steps, steps], axis=1)
    now = iota((TB, MOST_STEPS), 1).astype(f32)
    hit = ((start <= now) & (now < start + steps)).astype(f32)
    own_tile = jnp.sum(hit * iota((TB, MOST_STEPS), 0).astype(f32), axis=0, keepdims=True)
    within = jnp.sum(hit * (now - start), axis=0, keepdims=True)
    total = jnp.sum(steps, axis=0, keepdims=True)
    place_t = exact_dot(place.T, hit)
    gap_t = exact_dot(gap.T, hit)
    covered = jnp.sum(hit, axis=0, keepdims=True)
    tile = iota((128, MOST_STEPS), 0).astype(f32)
    rows = [own_tile, (within < 0.5).astype(f32), total]
    gaps = []
    for g in range(GROUP):
        chosen = ((place_t == within * GROUP + g) & (covered > 0.5)).astype(f32)
        present = jnp.sum(chosen, axis=0, keepdims=True)
        rows.append(jnp.sum(chosen * tile, axis=0, keepdims=True))
        gaps.append(jnp.where(present > 0.5, jnp.sum(chosen * gap_t, axis=0, keepdims=True), -1.0))
    rows = rows + gaps
    rows = rows + [jnp.zeros((1, MOST_STEPS), f32)] * (16 - len(rows))
    out_ref[...] = jnp.concatenate(rows, axis=0).astype(i32)


def table(block, perm, layer, mask):
    return pl.pallas_call(
        table_kernel,
        out_shape=jax.ShapeDtypeStruct((16, MOST_STEPS), i32),
        in_specs=[pl.BlockSpec(memory_space=pltpu.SMEM)] + [pl.BlockSpec(memory_space=pltpu.VMEM)] * 3,
        out_specs=pl.BlockSpec(memory_space=pltpu.VMEM),
        name="table",
    )(block, perm.reshape(1, TILES), layer.reshape(1, TILES), mask)


def attend_kernel(
    table_ref,
    slope_ref,
    q_ref,
    prior_ref,
    own_ref,
    later_ref,
    out_ref,
    kv,
    scores,
    weights,
    arrived,
):
    copies = [
        pltpu.make_async_copy(source, kv.at[pl.ds(index * TB, TB)], arrived.at[index])
        for index, source in enumerate((prior_ref, own_ref, later_ref))
    ]
    for copy in copies:
        copy.start()
    scale = EXPONENT / math.sqrt(HD)
    slope = slope_ref[0] * EXPONENT
    total_steps = table_ref[2, 0]
    zeros = jnp.zeros((HD, TILE), bf16)
    for copy in copies:
        copy.wait()

    def score(step):
        q = q_ref[table_ref[0, step]]
        q = jnp.concatenate(
            [jnp.concatenate([q, zeros], axis=1), jnp.concatenate([zeros, q], axis=1)], axis=0
        )
        k = jnp.concatenate([kv[table_ref[3 + g, step], :HD, :] for g in range(GROUP)], axis=0)
        scores[lax.rem(step, 2)] = jnp.dot(k, q, preferred_element_type=f32)

    def weigh(step, top, total):
        slot = lax.rem(step, 2)
        first = table_ref[1, step] == 1
        biases = []
        highest = None
        for g in range(GROUP):
            gap = table_ref[3 + GROUP + g, step]
            bias = jnp.where(gap < 0, -LOWEST, slope * gap.astype(f32))
            biases.append(bias)
            s = scores[slot, g * HD : g * HD + HD, :]
            s = jnp.maximum(s[:, :TILE], s[:, TILE:])
            s = jnp.max(s, axis=0, keepdims=True) * scale - bias
            highest = s if highest is None else jnp.maximum(highest, s)
        top = jnp.where(first, LOWEST, top)
        new_top = jnp.maximum(top, highest)
        fade = jnp.exp2(top - new_top)
        added = None
        for g in range(GROUP):
            s = scores[slot, g * HD : g * HD + HD, :]
            offset = new_top + biases[g]
            for half in range(2):
                w = jnp.exp2(s[:, half * TILE : half * TILE + TILE] * scale - offset)
                added = w if added is None else added + w
                row = g * TILE + half * HD
                weights[slot, row : row + HD, :] = w.astype(bf16)
        added = jnp.sum(added, axis=0, keepdims=True)
        total = jnp.where(first, 0.0, total * fade) + added
        return new_top, total, fade

    def gather(step, fade, total, mixed):
        slot = lax.rem(step, 2)
        first = table_ref[1, step] == 1
        v = jnp.concatenate([kv[table_ref[3 + g, step], HD:, :] for g in range(GROUP)], axis=1)
        mixed = jnp.where(first, 0.0, mixed * fade)
        mixed = mixed + jnp.dot(v, weights[slot], preferred_element_type=f32)
        out_ref[table_ref[0, step]] = (mixed / total).astype(bf16)
        return mixed

    def body(step, carry):
        top, total, fade, mixed = carry
        mixed = gather(jnp.maximum(step - 2, 0), fade, total, mixed)
        top, total, fade = weigh(jnp.maximum(step - 1, 0), top, total)
        score(step)
        return top, total, fade, mixed

    row = jnp.zeros((1, TILE), f32)
    scores[...] = jnp.zeros_like(scores)
    weights[...] = jnp.zeros_like(weights)
    lax.fori_loop(
        0, total_steps + 2, body, (row, row + 1.0, row, jnp.zeros((HD, TILE), f32))
    )


def attend(steps, slope, q, prior, own, later):
    smem = pl.BlockSpec(memory_space=pltpu.SMEM)
    vmem = pl.BlockSpec(memory_space=pltpu.VMEM)
    anywhere = pl.BlockSpec(memory_space=pl.ANY)
    return pl.pallas_call(
        attend_kernel,
        out_shape=jax.ShapeDtypeStruct((TB, HD, TILE), bf16),
        in_specs=[smem, smem, vmem, anywhere, anywhere, anywhere],
        out_specs=vmem,
        scratch_shapes=[
            pltpu.VMEM((3 * TB, 2 * HD, TILE), bf16),
            pltpu.VMEM((2, GROUP * HD, 2 * TILE), f32),
            pltpu.VMEM((2, GROUP * TILE, TILE), bf16),
            pltpu.SemaphoreType.DMA((3,)),
        ],
        name="attend",
    )(steps, slope, q, prior, own, later)


def exchange(array):
    return lax.all_to_all(array, "head", split_axis=0, concat_axis=0, tiled=True)


def per_device(queries, keys, values, slopes, layer, mask, perm):
    block = lax.axis_index("blk").astype(i32).reshape(1)
    slope = lax.dynamic_slice_in_dim(slopes, lax.axis_index("head"), 1)
    own = exchange(pack_kv(keys, values))
    prior = from_behind(own, "blk", 1)
    later = from_behind(own, "blk", -1)
    q = exchange(pack_q(queries))
    steps = table(block, perm, layer, mask)
    mixed = attend(steps, slope, q, prior, own, later)
    return unpack(exchange(mixed))


def solution(mesh):
    rows = P(("blk", "head"), None)
    return jax.shard_map(
        per_device,
        mesh=mesh,
        in_specs=(rows, rows, rows, P(), P(), P(), P()),
        out_specs=rows,
        check_vma=False,
    )
```

```python
import math

import jax
import jax.numpy as jnp
from jax import lax
from jax.experimental import pallas as pl
from jax.experimental.pallas import tpu as pltpu
from jax.sharding import PartitionSpec as P

HD = 64
HEADS = 32
TILE = 128
TB = 32
TILES = 256
KCAP = 9
GROUP = 3
UNROLL = 3
MOST_STEPS = 256
LOWEST = -1e30
EXPONENT = math.log2(math.e)

f32 = jnp.float32
bf16 = jnp.bfloat16
i32 = jnp.int32


def from_behind(value, axis, steps):
    count = lax.axis_size(axis)
    pairs = [(source, (source + steps) % count) for source in range(count)]
    return lax.ppermute(value, axis, pairs)


def pack_kv_kernel(k_ref, v_ref, kv_ref):
    for pair in range(HEADS // 2):
        columns = slice(pair * 128, pair * 128 + 128)
        k = k_ref[:, columns]
        upper, lower = k[:64], k[64:]
        kv_ref[2 * pair, :64, :] = jnp.concatenate([upper[:, :64], lower[:, :64]], axis=1)
        kv_ref[2 * pair + 1, :64, :] = jnp.concatenate([upper[:, 64:], lower[:, 64:]], axis=1)
        v = v_ref[:, columns].T
        kv_ref[2 * pair, 64:, :] = v[:64]
        kv_ref[2 * pair + 1, 64:, :] = v[64:]


def pack_kv(keys, values):
    return pl.pallas_call(
        pack_kv_kernel,
        out_shape=jax.ShapeDtypeStruct((HEADS, 128, 128), bf16),
        name="pack_kv",
    )(keys, values)


def pack_q_kernel(q_ref, out_ref):
    for pair in range(HEADS // 2):
        q = q_ref[:, pair * 128 : pair * 128 + 128].T
        out_ref[2 * pair] = q[:64]
        out_ref[2 * pair + 1] = q[64:]


def pack_q(queries):
    return pl.pallas_call(
        pack_q_kernel,
        out_shape=jax.ShapeDtypeStruct((HEADS, HD, 128), bf16),
        name="pack_q",
    )(queries)


def unpack_kernel(in_ref, out_ref):
    for pair in range(HEADS // 2):
        both = jnp.concatenate([in_ref[2 * pair], in_ref[2 * pair + 1]], axis=0)
        out_ref[:, pair * 128 : pair * 128 + 128] = both.T


def unpack(array):
    return pl.pallas_call(
        unpack_kernel,
        out_shape=jax.ShapeDtypeStruct((128, HEADS * HD), bf16),
        name="unpack",
    )(array)


def iota(shape, dim):
    return lax.broadcasted_iota(i32, shape, dim)


def exact_dot(a, b):
    return jnp.dot(a.astype(bf16), b.astype(bf16), preferred_element_type=f32)


def table_kernel(block_ref, perm_ref, layer_ref, mask_ref, out_ref):
    block = block_ref[0]
    shift = lax.rem(TILES + TB - block * TB, TILES)
    perm = pltpu.roll(jnp.broadcast_to(perm_ref[...], (8, TILES)), shift, 1)[:1, :128]
    select = (perm == iota((TILES, 128), 0)).astype(f32)
    select_t = select.T
    own_select = select_t[TB : 2 * TB]
    columns = exact_dot(mask_ref[...].astype(f32), select)
    allowed = exact_dot(own_select, columns)
    allowed = jnp.where(iota((TB, 128), 1) < 3 * TB, allowed, 0.0)
    layer = layer_ref[...].astype(f32)
    layer_row = exact_dot(jnp.broadcast_to(layer, (8, TILES)), select)[:1]
    layer_own = jnp.sum(own_select * layer, axis=1, keepdims=True)
    gap = jnp.abs(layer_own - layer_row)
    before = (iota((128, 128), 0) < iota((128, 128), 1)).astype(f32)
    place = exact_dot(allowed, before)
    place = jnp.where(allowed > 0.5, place, 200.0)
    count = jnp.sum(allowed, axis=1, keepdims=True)
    steps = jnp.zeros((TB, 1), f32)
    for filled in range(0, 3 * KCAP, GROUP):
        steps = steps + (count > filled + 0.5).astype(f32)
    steps = jnp.broadcast_to(steps, (TB, 128))
    earlier = (iota((TB, TB), 1) < iota((TB, TB), 0)).astype(f32)
    start = exact_dot(earlier, steps)
    start = jnp.concatenate([start, start], axis=1)
    steps = jnp.concatenate([steps, steps], axis=1)
    now = iota((TB, MOST_STEPS), 1).astype(f32)
    hit = ((start <= now) & (now < start + steps)).astype(f32)
    covered = jnp.sum(hit, axis=0, keepdims=True)
    own_tile = jnp.sum(hit * iota((TB, MOST_STEPS), 0).astype(f32), axis=0, keepdims=True)
    own_tile = jnp.where(covered > 0.5, own_tile, TB - 1.0)
    within = jnp.sum(hit * (now - start), axis=0, keepdims=True)
    opening = (covered > 0.5) & (within < 0.5)
    total = jnp.sum(steps, axis=0, keepdims=True)
    place_t = exact_dot(place.T, hit)
    gap_t = exact_dot(gap.T, hit)
    tile = iota((128, MOST_STEPS), 0).astype(f32)
    rows = [own_tile, opening.astype(f32), total]
    gaps = []
    for g in range(GROUP):
        chosen = ((place_t == within * GROUP + g) & (covered > 0.5)).astype(f32)
        present = jnp.sum(chosen, axis=0, keepdims=True)
        rows.append(jnp.sum(chosen * tile, axis=0, keepdims=True))
        gaps.append(jnp.where(present > 0.5, jnp.sum(chosen * gap_t, axis=0, keepdims=True), -1.0))
    rows = rows + gaps
    rows = rows + [jnp.zeros((1, MOST_STEPS), f32)] * (16 - len(rows))
    out_ref[...] = jnp.concatenate(rows, axis=0).astype(i32)


def table(block, perm, layer, mask):
    return pl.pallas_call(
        table_kernel,
        out_shape=jax.ShapeDtypeStruct((16, MOST_STEPS), i32),
        in_specs=[pl.BlockSpec(memory_space=pltpu.SMEM)] + [pl.BlockSpec(memory_space=pltpu.VMEM)] * 3,
        out_specs=pl.BlockSpec(memory_space=pltpu.VMEM),
        name="table",
    )(block, perm.reshape(1, TILES), layer.reshape(1, TILES), mask)


def attend_kernel(
    table_ref,
    slope_ref,
    q_ref,
    prior_ref,
    own_ref,
    later_ref,
    out_ref,
    kv,
    arrived,
    *buffers,
):
    scores, weights = buffers[: 2 * UNROLL], buffers[2 * UNROLL :]
    copies = [
        pltpu.make_async_copy(source, kv.at[pl.ds(index * TB, TB)], arrived.at[index])
        for index, source in enumerate((prior_ref, own_ref, later_ref))
    ]
    for copy in copies:
        copy.start()
    scale = EXPONENT / math.sqrt(HD)
    slope = slope_ref[0] * EXPONENT
    total_steps = table_ref[2, 0]
    zeros = jnp.zeros((HD, TILE), bf16)
    for copy in copies:
        copy.wait()

    def score(step, into):
        q = q_ref[table_ref[0, step]]
        q = jnp.concatenate(
            [jnp.concatenate([q, zeros], axis=1), jnp.concatenate([zeros, q], axis=1)], axis=0
        )
        k = jnp.concatenate([kv[table_ref[3 + g, step], :HD, :] for g in range(GROUP)], axis=0)
        into[...] = jnp.dot(k, q, preferred_element_type=f32)

    def weigh(step, source, into, top):
        first = table_ref[1, step] == 1
        biases = []
        top = jnp.where(first, LOWEST, top)
        new_top = top
        for g in range(GROUP):
            gap = table_ref[3 + GROUP + g, step]
            biases.append(jnp.where(gap < 0, -LOWEST, slope * gap.astype(f32)))
            s = source[g * HD : g * HD + HD, :]
            s = jnp.maximum(s[:, :TILE], s[:, TILE:])
            s = jnp.max(s, axis=0, keepdims=True) * scale - biases[g]
            new_top = jnp.maximum(new_top, s)
        for g in range(GROUP):
            s = source[g * HD : g * HD + HD, :]
            offset = new_top + biases[g]
            for half in range(2):
                w = jnp.exp2(s[:, half * TILE : half * TILE + TILE] * scale - offset)
                row = g * TILE + half * HD
                into[row : row + HD, :] = w.astype(bf16)
        return new_top, jnp.where(first, 0.0, jnp.exp2(top - new_top))

    def gather(step, source, fade, mixed):
        v = jnp.concatenate([kv[table_ref[3 + g, step], HD:, :] for g in range(GROUP)], axis=1)
        v = jnp.concatenate([v, ones], axis=0)
        mixed = mixed * fade + jnp.dot(v, source[...], preferred_element_type=f32)
        out_ref[table_ref[0, step]] = (mixed[:HD] * (1.0 / mixed[HD : HD + 1])).astype(bf16)
        return mixed

    def body(pair, carry):
        top, mixed, fades = carry
        for parity in range(2):
            trip = pair * 2 + parity
            for u in range(UNROLL):
                step = jnp.maximum((trip - 2) * UNROLL + u, 0)
                mixed = gather(step, weights[parity * UNROLL + u], fades[parity * UNROLL + u], mixed)
            for u in range(UNROLL):
                step = jnp.maximum((trip - 1) * UNROLL + u, 0)
                slot = (1 - parity) * UNROLL + u
                top, fade = weigh(step, scores[slot], weights[slot], top)
                fades = fades[:slot] + (fade,) + fades[slot + 1 :]
            for u in range(UNROLL):
                score(trip * UNROLL + u, scores[parity * UNROLL + u])
        return top, mixed, fades

    row = jnp.zeros((1, TILE), f32)
    ones = jnp.ones((16, GROUP * TILE), bf16)
    for slot in range(UNROLL, 2 * UNROLL):
        scores[slot][...] = jnp.zeros_like(scores[slot])
    for ref in weights:
        ref[...] = jnp.zeros_like(ref)
    pairs = lax.div(total_steps + 4 * UNROLL - 1, 2 * UNROLL)
    lax.fori_loop(0, pairs, body, (row, jnp.zeros((HD + 16, TILE), f32), (row,) * (2 * UNROLL)))


def attend(steps, slope, q, prior, own, later):
    smem = pl.BlockSpec(memory_space=pltpu.SMEM)
    vmem = pl.BlockSpec(memory_space=pltpu.VMEM)
    anywhere = pl.BlockSpec(memory_space=pl.ANY)
    return pl.pallas_call(
        attend_kernel,
        out_shape=jax.ShapeDtypeStruct((TB, HD, TILE), bf16),
        in_specs=[smem, smem, vmem, anywhere, anywhere, anywhere],
        out_specs=vmem,
        scratch_shapes=[
            pltpu.VMEM((3 * TB, 2 * HD, TILE), bf16),
            pltpu.SemaphoreType.DMA((3,)),
        ]
        + [pltpu.VMEM((GROUP * HD, 2 * TILE), f32)] * (2 * UNROLL)
        + [pltpu.VMEM((GROUP * TILE, TILE), bf16)] * (2 * UNROLL),
        name="attend",
    )(steps, slope, q, prior, own, later)


def exchange(array):
    return lax.all_to_all(array, "head", split_axis=0, concat_axis=0, tiled=True)


def per_device(queries, keys, values, slopes, layer, mask, perm):
    block = lax.axis_index("blk").astype(i32).reshape(1)
    slope = lax.dynamic_slice_in_dim(slopes, lax.axis_index("head"), 1)
    own = exchange(pack_kv(keys, values))
    packed = pack_q(queries)
    steps = table(block, perm, layer, mask)
    own, packed, steps = lax.optimization_barrier((own, packed, steps))
    prior = from_behind(own, "blk", 1)
    later = from_behind(own, "blk", -1)
    q = exchange(packed)
    mixed = attend(steps, slope, q, prior, own, later)
    return unpack(exchange(mixed))


def solution(mesh):
    rows = P(("blk", "head"), None)
    return jax.shard_map(
        per_device,
        mesh=mesh,
        in_specs=(rows, rows, rows, P(), P(), P(), P()),
        out_specs=rows,
        check_vma=False,
    )
```

```python
import math

import jax
import jax.numpy as jnp
from jax import lax
from jax.experimental import pallas as pl
from jax.experimental.pallas import tpu as pltpu
from jax.sharding import PartitionSpec as P

HD = 64
HEADS = 32
TILE = 128
TB = 32
TILES = 256
KCAP = 9
GROUP = 3
UNROLL = 3
PARTS = 2
MOST_STEPS = 256
LOWEST = -1e30
EXPONENT = math.log2(math.e)

f32 = jnp.float32
bf16 = jnp.bfloat16
i32 = jnp.int32


def from_behind(value, axis, steps):
    count = lax.axis_size(axis)
    pairs = [(source, (source + steps) % count) for source in range(count)]
    return lax.ppermute(value, axis, pairs)


def pack_kv_kernel(k_hbm, v_hbm, kv_hbm, k_ref, v_ref, kv_ref, k_sem, v_sem, kv_sem):
    width = HEADS * HD // PARTS
    heads = HEADS // PARTS
    loads, stores = [], []
    for part in range(PARTS):
        columns = pl.ds(part * width, width)
        k_load = pltpu.make_async_copy(k_hbm.at[:, columns], k_ref.at[part], k_sem.at[part])
        v_load = pltpu.make_async_copy(v_hbm.at[:, columns], v_ref.at[part], v_sem.at[part])
        k_load.start()
        v_load.start()
        loads.append((k_load, v_load))
    for part in range(PARTS):
        loads[part][0].wait()
        loads[part][1].wait()
        for pair in range(heads // 2):
            columns = slice(pair * 128, pair * 128 + 128)
            one, two = part * heads + 2 * pair, part * heads + 2 * pair + 1
            k = k_ref[part, :, columns]
            upper, lower = k[:64], k[64:]
            kv_ref[one, :64, :] = jnp.concatenate([upper[:, :64], lower[:, :64]], axis=1)
            kv_ref[two, :64, :] = jnp.concatenate([upper[:, 64:], lower[:, 64:]], axis=1)
            v = v_ref[part, :, columns].T
            kv_ref[one, 64:, :] = v[:64]
            kv_ref[two, 64:, :] = v[64:]
        chunk = pl.ds(part * heads, heads)
        store = pltpu.make_async_copy(kv_ref.at[chunk], kv_hbm.at[chunk], kv_sem.at[part])
        store.start()
        stores.append(store)
    for store in stores:
        store.wait()


def pack_kv(keys, values):
    anywhere = pl.BlockSpec(memory_space=pl.ANY)
    return pl.pallas_call(
        pack_kv_kernel,
        out_shape=jax.ShapeDtypeStruct((HEADS, 128, 128), bf16),
        in_specs=[anywhere] * 2,
        out_specs=anywhere,
        scratch_shapes=[pltpu.VMEM((PARTS, 128, HEADS * HD // PARTS), bf16)] * 2
        + [pltpu.VMEM((HEADS, 128, 128), bf16)]
        + [pltpu.SemaphoreType.DMA((PARTS,))] * 3,
        name="pack_kv",
    )(keys, values)


def pack_q_kernel(q_ref, out_ref):
    for pair in range(HEADS // 2):
        q = q_ref[:, pair * 128 : pair * 128 + 128].T
        out_ref[2 * pair] = q[:64]
        out_ref[2 * pair + 1] = q[64:]


def pack_q(queries):
    return pl.pallas_call(
        pack_q_kernel,
        out_shape=jax.ShapeDtypeStruct((HEADS, HD, 128), bf16),
        name="pack_q",
    )(queries)


def unpack_kernel(in_ref, out_ref):
    for pair in range(HEADS // 2):
        both = jnp.concatenate([in_ref[2 * pair], in_ref[2 * pair + 1]], axis=0)
        out_ref[:, pair * 128 : pair * 128 + 128] = both.T


def unpack(array):
    return pl.pallas_call(
        unpack_kernel,
        out_shape=jax.ShapeDtypeStruct((128, HEADS * HD), bf16),
        compiler_params=pltpu.CompilerParams(vmem_limit_bytes=8 * 2**20),
        name="unpack",
    )(array)


def iota(shape, dim):
    return lax.broadcasted_iota(i32, shape, dim)


def exact_dot(a, b):
    return jnp.dot(a.astype(bf16), b.astype(bf16), preferred_element_type=f32)


def table_kernel(block_ref, perm_ref, layer_ref, mask_ref, out_ref):
    block = block_ref[0]
    shift = lax.rem(TILES + TB - block * TB, TILES)
    perm = pltpu.roll(jnp.broadcast_to(perm_ref[...], (8, TILES)), shift, 1)[:1, :128]
    select = (perm == iota((TILES, 128), 0)).astype(f32)
    select_t = select.T
    own_select = select_t[TB : 2 * TB]
    columns = exact_dot(mask_ref[...].astype(f32), select)
    allowed = exact_dot(own_select, columns)
    allowed = jnp.where(iota((TB, 128), 1) < 3 * TB, allowed, 0.0)
    layer = layer_ref[...].astype(f32)
    layer_row = exact_dot(jnp.broadcast_to(layer, (8, TILES)), select)[:1]
    layer_own = jnp.sum(own_select * layer, axis=1, keepdims=True)
    gap = jnp.abs(layer_own - layer_row)
    before = (iota((128, 128), 0) < iota((128, 128), 1)).astype(f32)
    place = exact_dot(allowed, before)
    place = jnp.where(allowed > 0.5, place, 200.0)
    count = jnp.sum(allowed, axis=1, keepdims=True)
    steps = jnp.zeros((TB, 1), f32)
    for filled in range(0, 3 * KCAP, GROUP):
        steps = steps + (count > filled + 0.5).astype(f32)
    steps = jnp.broadcast_to(steps, (TB, 128))
    earlier = (iota((TB, TB), 1) < iota((TB, TB), 0)).astype(f32)
    start = exact_dot(earlier, steps)
    start = jnp.concatenate([start, start], axis=1)
    steps = jnp.concatenate([steps, steps], axis=1)
    now = iota((TB, MOST_STEPS), 1).astype(f32)
    hit = ((start <= now) & (now < start + steps)).astype(f32)
    covered = jnp.sum(hit, axis=0, keepdims=True)
    own_tile = jnp.sum(hit * iota((TB, MOST_STEPS), 0).astype(f32), axis=0, keepdims=True)
    own_tile = jnp.where(covered > 0.5, own_tile, TB - 1.0)
    within = jnp.sum(hit * (now - start), axis=0, keepdims=True)
    opening = (covered > 0.5) & (within < 0.5)
    total = jnp.sum(steps, axis=0, keepdims=True)
    place_t = exact_dot(place.T, hit)
    gap_t = exact_dot(gap.T, hit)
    tile = iota((128, MOST_STEPS), 0).astype(f32)
    rows = [own_tile, opening.astype(f32), total]
    gaps = []
    for g in range(GROUP):
        chosen = ((place_t == within * GROUP + g) & (covered > 0.5)).astype(f32)
        present = jnp.sum(chosen, axis=0, keepdims=True)
        rows.append(jnp.sum(chosen * tile, axis=0, keepdims=True))
        gaps.append(jnp.where(present > 0.5, jnp.sum(chosen * gap_t, axis=0, keepdims=True), -1.0))
    rows = rows + gaps
    rows = rows + [jnp.zeros((1, MOST_STEPS), f32)] * (16 - len(rows))
    out_ref[...] = jnp.concatenate(rows, axis=0).astype(i32)


def table(block, perm, layer, mask):
    return pl.pallas_call(
        table_kernel,
        out_shape=jax.ShapeDtypeStruct((16, MOST_STEPS), i32),
        in_specs=[pl.BlockSpec(memory_space=pltpu.SMEM)] + [pl.BlockSpec(memory_space=pltpu.VMEM)] * 3,
        out_specs=pl.BlockSpec(memory_space=pltpu.VMEM),
        name="table",
    )(block, perm.reshape(1, TILES), layer.reshape(1, TILES), mask)


def attend_kernel(
    table_ref,
    slope_ref,
    q_ref,
    prior_ref,
    own_ref,
    later_ref,
    out_ref,
    kv,
    arrived,
    *buffers,
):
    scores, weights = buffers[: 2 * UNROLL], buffers[2 * UNROLL :]
    copies = [
        pltpu.make_async_copy(source, kv.at[pl.ds(index * TB, TB)], arrived.at[index])
        for index, source in enumerate((prior_ref, own_ref, later_ref))
    ]
    for copy in copies:
        copy.start()
    scale = EXPONENT / math.sqrt(HD)
    slope = slope_ref[0] * EXPONENT
    total_steps = table_ref[2, 0]
    zeros = jnp.zeros((HD, TILE), bf16)
    for copy in copies:
        copy.wait()

    def score(step, into):
        q = q_ref[table_ref[0, step]]
        q = jnp.concatenate(
            [jnp.concatenate([q, zeros], axis=1), jnp.concatenate([zeros, q], axis=1)], axis=0
        )
        k = jnp.concatenate([kv[table_ref[3 + g, step], :HD, :] for g in range(GROUP)], axis=0)
        into[...] = jnp.dot(k, q, preferred_element_type=f32)

    def weigh(step, source, into, top):
        first = table_ref[1, step] == 1
        biases = []
        top = jnp.where(first, LOWEST, top)
        new_top = top
        for g in range(GROUP):
            gap = table_ref[3 + GROUP + g, step]
            biases.append(jnp.where(gap < 0, -LOWEST, slope * gap.astype(f32)))
            s = source[g * HD : g * HD + HD, :]
            s = jnp.maximum(s[:, :TILE], s[:, TILE:])
            s = jnp.max(s, axis=0, keepdims=True) * scale - biases[g]
            new_top = jnp.maximum(new_top, s)
        for g in range(GROUP):
            s = source[g * HD : g * HD + HD, :]
            offset = new_top + biases[g]
            for half in range(2):
                w = jnp.exp2(s[:, half * TILE : half * TILE + TILE] * scale - offset)
                row = g * TILE + half * HD
                into[row : row + HD, :] = w.astype(bf16)
        return new_top, jnp.where(first, 0.0, jnp.exp2(top - new_top))

    def gather(step, source, fade, mixed):
        v = jnp.concatenate([kv[table_ref[3 + g, step], HD:, :] for g in range(GROUP)], axis=1)
        v = jnp.concatenate([v, ones], axis=0)
        mixed = mixed * fade + jnp.dot(v, source[...], preferred_element_type=f32)
        out_ref[table_ref[0, step]] = (mixed[:HD] * (1.0 / mixed[HD : HD + 1])).astype(bf16)
        return mixed

    def body(pair, carry):
        top, mixed, fades = carry
        for parity in range(2):
            trip = pair * 2 + parity
            for u in range(UNROLL):
                step = jnp.maximum((trip - 2) * UNROLL + u, 0)
                mixed = gather(step, weights[parity * UNROLL + u], fades[parity * UNROLL + u], mixed)
            for u in range(UNROLL):
                step = jnp.maximum((trip - 1) * UNROLL + u, 0)
                slot = (1 - parity) * UNROLL + u
                top, fade = weigh(step, scores[slot], weights[slot], top)
                fades = fades[:slot] + (fade,) + fades[slot + 1 :]
            for u in range(UNROLL):
                score(trip * UNROLL + u, scores[parity * UNROLL + u])
        return top, mixed, fades

    row = jnp.zeros((1, TILE), f32)
    ones = jnp.ones((16, GROUP * TILE), bf16)
    for slot in range(UNROLL, 2 * UNROLL):
        scores[slot][...] = jnp.zeros_like(scores[slot])
    for ref in weights:
        ref[...] = jnp.zeros_like(ref)
    pairs = lax.div(total_steps + 4 * UNROLL - 1, 2 * UNROLL)
    lax.fori_loop(0, pairs, body, (row, jnp.zeros((HD + 16, TILE), f32), (row,) * (2 * UNROLL)))


def attend(steps, slope, q, prior, own, later):
    smem = pl.BlockSpec(memory_space=pltpu.SMEM)
    vmem = pl.BlockSpec(memory_space=pltpu.VMEM)
    anywhere = pl.BlockSpec(memory_space=pl.ANY)
    return pl.pallas_call(
        attend_kernel,
        out_shape=jax.ShapeDtypeStruct((TB, HD, TILE), bf16),
        in_specs=[smem, smem, vmem, anywhere, anywhere, anywhere],
        out_specs=vmem,
        scratch_shapes=[
            pltpu.VMEM((3 * TB, 2 * HD, TILE), bf16),
            pltpu.SemaphoreType.DMA((3,)),
        ]
        + [pltpu.VMEM((GROUP * HD, 2 * TILE), f32)] * (2 * UNROLL)
        + [pltpu.VMEM((GROUP * TILE, TILE), bf16)] * (2 * UNROLL),
        compiler_params=pltpu.CompilerParams(vmem_limit_bytes=12 * 2**20),
        name="attend",
    )(steps, slope, q, prior, own, later)


def exchange(array):
    return lax.all_to_all(array, "head", split_axis=0, concat_axis=0, tiled=True)


def per_device(queries, keys, values, slopes, layer, mask, perm):
    block = lax.axis_index("blk").astype(i32).reshape(1)
    slope = lax.dynamic_slice_in_dim(slopes, lax.axis_index("head"), 1)
    own = exchange(pack_kv(keys, values))
    packed = pack_q(queries)
    steps = table(block, perm, layer, mask)
    own, packed, steps = lax.optimization_barrier((own, packed, steps))
    prior = from_behind(own, "blk", 1)
    later = from_behind(own, "blk", -1)
    q = exchange(packed)
    mixed = attend(steps, slope, q, prior, own, later)
    return unpack(exchange(mixed))


def solution(mesh):
    rows = P(("blk", "head"), None)
    return jax.shard_map(
        per_device,
        mesh=mesh,
        in_specs=(rows, rows, rows, P(), P(), P(), P()),
        out_specs=rows,
        check_vma=False,
    )
```

```python
import math

import jax
import jax.numpy as jnp
from jax import lax
from jax.experimental import pallas as pl
from jax.experimental.pallas import tpu as pltpu
from jax.sharding import PartitionSpec as P

HD = 64
HEADS = 32
TILE = 128
TB = 32
TILES = 256
KCAP = 9
GROUP = 3
UNROLL = 3
PARTS = 2
MOST_STEPS = 256
LOWEST = -1e30
EXPONENT = math.log2(math.e)

f32 = jnp.float32
bf16 = jnp.bfloat16
i32 = jnp.int32


def place_of(head, swap):
    if head % 2 == 0:
        return head
    return head - swap if head & 2 else head + swap


def from_behind(value, steps):
    blocks, heads = lax.axis_size("blk"), lax.axis_size("head")
    pairs = []
    for block in range(blocks):
        target = (block + steps) % blocks
        crosses = 2 * block // blocks != 2 * target // blocks
        for place in range(heads):
            other = place ^ 2 if crosses and place % 2 else place
            pairs.append((block * heads + place, target * heads + other))
    return lax.ppermute(value, ("blk", "head"), pairs)


def pack_kv_kernel(swap_ref, k_hbm, v_hbm, kv_hbm, k_ref, v_ref, kv_ref, k_sem, v_sem, kv_sem):
    width = HEADS * HD // PARTS
    heads = HEADS // PARTS
    loads, stores = [], []
    for part in range(PARTS):
        columns = pl.ds(part * width, width)
        k_load = pltpu.make_async_copy(k_hbm.at[:, columns], k_ref.at[part], k_sem.at[part])
        v_load = pltpu.make_async_copy(v_hbm.at[:, columns], v_ref.at[part], v_sem.at[part])
        k_load.start()
        v_load.start()
        loads.append((k_load, v_load))
    for part in range(PARTS):
        loads[part][0].wait()
        loads[part][1].wait()
        for pair in range(heads // 2):
            columns = slice(pair * 128, pair * 128 + 128)
            one = part * heads + 2 * pair
            two = place_of(one + 1, swap_ref[0])
            k = k_ref[part, :, columns]
            upper, lower = k[:64], k[64:]
            kv_ref[one, :64, :] = jnp.concatenate([upper[:, :64], lower[:, :64]], axis=1)
            kv_ref[two, :64, :] = jnp.concatenate([upper[:, 64:], lower[:, 64:]], axis=1)
            v = v_ref[part, :, columns].T
            kv_ref[one, 64:, :] = v[:64]
            kv_ref[two, 64:, :] = v[64:]
        chunk = pl.ds(part * heads, heads)
        store = pltpu.make_async_copy(kv_ref.at[chunk], kv_hbm.at[chunk], kv_sem.at[part])
        store.start()
        stores.append(store)
    for store in stores:
        store.wait()


def pack_kv(swap, keys, values):
    anywhere = pl.BlockSpec(memory_space=pl.ANY)
    return pl.pallas_call(
        pack_kv_kernel,
        out_shape=jax.ShapeDtypeStruct((HEADS, 128, 128), bf16),
        in_specs=[pl.BlockSpec(memory_space=pltpu.SMEM)] + [anywhere] * 2,
        out_specs=anywhere,
        scratch_shapes=[pltpu.VMEM((PARTS, 128, HEADS * HD // PARTS), bf16)] * 2
        + [pltpu.VMEM((HEADS, 128, 128), bf16)]
        + [pltpu.SemaphoreType.DMA((PARTS,))] * 3,
        name="pack_kv",
    )(swap, keys, values)


def pack_q_kernel(swap_ref, q_ref, out_ref):
    for pair in range(HEADS // 2):
        q = q_ref[:, pair * 128 : pair * 128 + 128].T
        out_ref[2 * pair] = q[:64]
        out_ref[place_of(2 * pair + 1, swap_ref[0])] = q[64:]


def pack_q(swap, queries):
    return pl.pallas_call(
        pack_q_kernel,
        out_shape=jax.ShapeDtypeStruct((HEADS, HD, 128), bf16),
        in_specs=[pl.BlockSpec(memory_space=pltpu.SMEM), pl.BlockSpec(memory_space=pltpu.VMEM)],
        out_specs=pl.BlockSpec(memory_space=pltpu.VMEM),
        name="pack_q",
    )(swap, queries)


def unpack_kernel(swap_ref, in_ref, out_ref):
    for pair in range(HEADS // 2):
        two = place_of(2 * pair + 1, swap_ref[0])
        both = jnp.concatenate([in_ref[2 * pair], in_ref[two]], axis=0)
        out_ref[:, pair * 128 : pair * 128 + 128] = both.T


def unpack(swap, array):
    return pl.pallas_call(
        unpack_kernel,
        out_shape=jax.ShapeDtypeStruct((128, HEADS * HD), bf16),
        in_specs=[pl.BlockSpec(memory_space=pltpu.SMEM), pl.BlockSpec(memory_space=pltpu.VMEM)],
        out_specs=pl.BlockSpec(memory_space=pltpu.VMEM),
        compiler_params=pltpu.CompilerParams(vmem_limit_bytes=8 * 2**20),
        name="unpack",
    )(swap, array)


def iota(shape, dim):
    return lax.broadcasted_iota(i32, shape, dim)


def exact_dot(a, b):
    return jnp.dot(a.astype(bf16), b.astype(bf16), preferred_element_type=f32)


def table_kernel(block_ref, perm_ref, layer_ref, mask_ref, out_ref):
    block = block_ref[0]
    shift = lax.rem(TILES + TB - block * TB, TILES)
    perm = pltpu.roll(jnp.broadcast_to(perm_ref[...], (8, TILES)), shift, 1)[:1, :128]
    select = (perm == iota((TILES, 128), 0)).astype(f32)
    select_t = select.T
    own_select = select_t[TB : 2 * TB]
    columns = exact_dot(mask_ref[...].astype(f32), select)
    allowed = exact_dot(own_select, columns)
    allowed = jnp.where(iota((TB, 128), 1) < 3 * TB, allowed, 0.0)
    layer = layer_ref[...].astype(f32)
    layer_row = exact_dot(jnp.broadcast_to(layer, (8, TILES)), select)[:1]
    layer_own = jnp.sum(own_select * layer, axis=1, keepdims=True)
    gap = jnp.abs(layer_own - layer_row)
    before = (iota((128, 128), 0) < iota((128, 128), 1)).astype(f32)
    place = exact_dot(allowed, before)
    place = jnp.where(allowed > 0.5, place, 200.0)
    count = jnp.sum(allowed, axis=1, keepdims=True)
    steps = jnp.zeros((TB, 1), f32)
    for filled in range(0, 3 * KCAP, GROUP):
        steps = steps + (count > filled + 0.5).astype(f32)
    steps = jnp.broadcast_to(steps, (TB, 128))
    earlier = (iota((TB, TB), 1) < iota((TB, TB), 0)).astype(f32)
    start = exact_dot(earlier, steps)
    start = jnp.concatenate([start, start], axis=1)
    steps = jnp.concatenate([steps, steps], axis=1)
    now = iota((TB, MOST_STEPS), 1).astype(f32)
    hit = ((start <= now) & (now < start + steps)).astype(f32)
    covered = jnp.sum(hit, axis=0, keepdims=True)
    own_tile = jnp.sum(hit * iota((TB, MOST_STEPS), 0).astype(f32), axis=0, keepdims=True)
    own_tile = jnp.where(covered > 0.5, own_tile, TB - 1.0)
    within = jnp.sum(hit * (now - start), axis=0, keepdims=True)
    opening = (covered > 0.5) & (within < 0.5)
    total = jnp.sum(steps, axis=0, keepdims=True)
    place_t = exact_dot(place.T, hit)
    gap_t = exact_dot(gap.T, hit)
    tile = iota((128, MOST_STEPS), 0).astype(f32)
    rows = [own_tile, opening.astype(f32), total]
    gaps = []
    for g in range(GROUP):
        chosen = ((place_t == within * GROUP + g) & (covered > 0.5)).astype(f32)
        present = jnp.sum(chosen, axis=0, keepdims=True)
        rows.append(jnp.sum(chosen * tile, axis=0, keepdims=True))
        gaps.append(jnp.where(present > 0.5, jnp.sum(chosen * gap_t, axis=0, keepdims=True), -1.0))
    rows = rows + gaps
    rows = rows + [jnp.zeros((1, MOST_STEPS), f32)] * (16 - len(rows))
    out_ref[...] = jnp.concatenate(rows, axis=0).astype(i32)


def table(block, perm, layer, mask):
    return pl.pallas_call(
        table_kernel,
        out_shape=jax.ShapeDtypeStruct((16, MOST_STEPS), i32),
        in_specs=[pl.BlockSpec(memory_space=pltpu.SMEM)] + [pl.BlockSpec(memory_space=pltpu.VMEM)] * 3,
        out_specs=pl.BlockSpec(memory_space=pltpu.VMEM),
        name="table",
    )(block, perm.reshape(1, TILES), layer.reshape(1, TILES), mask)


def attend_kernel(
    table_ref,
    slope_ref,
    q_ref,
    prior_ref,
    own_ref,
    later_ref,
    out_ref,
    kv,
    arrived,
    *buffers,
):
    scores, weights = buffers[: 2 * UNROLL], buffers[2 * UNROLL :]
    copies = [
        pltpu.make_async_copy(source, kv.at[pl.ds(index * TB, TB)], arrived.at[index])
        for index, source in enumerate((prior_ref, own_ref, later_ref))
    ]
    for copy in copies:
        copy.start()
    scale = EXPONENT / math.sqrt(HD)
    slope = slope_ref[0] * EXPONENT
    total_steps = table_ref[2, 0]
    zeros = jnp.zeros((HD, TILE), bf16)
    for copy in copies:
        copy.wait()

    def score(step, into):
        q = q_ref[table_ref[0, step]]
        q = jnp.concatenate(
            [jnp.concatenate([q, zeros], axis=1), jnp.concatenate([zeros, q], axis=1)], axis=0
        )
        k = jnp.concatenate([kv[table_ref[3 + g, step], :HD, :] for g in range(GROUP)], axis=0)
        into[...] = jnp.dot(k, q, preferred_element_type=f32)

    def weigh(step, source, into, top):
        first = table_ref[1, step] == 1
        biases = []
        top = jnp.where(first, LOWEST, top)
        new_top = top
        for g in range(GROUP):
            gap = table_ref[3 + GROUP + g, step]
            biases.append(jnp.where(gap < 0, -LOWEST, slope * gap.astype(f32)))
            s = source[g * HD : g * HD + HD, :]
            s = jnp.maximum(s[:, :TILE], s[:, TILE:])
            s = jnp.max(s, axis=0, keepdims=True) * scale - biases[g]
            new_top = jnp.maximum(new_top, s)
        for g in range(GROUP):
            s = source[g * HD : g * HD + HD, :]
            offset = new_top + biases[g]
            for half in range(2):
                w = jnp.exp2(s[:, half * TILE : half * TILE + TILE] * scale - offset)
                row = g * TILE + half * HD
                into[row : row + HD, :] = w.astype(bf16)
        return new_top, jnp.where(first, 0.0, jnp.exp2(top - new_top))

    def gather(step, source, fade, mixed):
        v = jnp.concatenate([kv[table_ref[3 + g, step], HD:, :] for g in range(GROUP)], axis=1)
        v = jnp.concatenate([v, ones], axis=0)
        mixed = mixed * fade + jnp.dot(v, source[...], preferred_element_type=f32)
        out_ref[table_ref[0, step]] = (mixed[:HD] * (1.0 / mixed[HD : HD + 1])).astype(bf16)
        return mixed

    def body(pair, carry):
        top, mixed, fades = carry
        for parity in range(2):
            trip = pair * 2 + parity
            for u in range(UNROLL):
                step = jnp.maximum((trip - 2) * UNROLL + u, 0)
                mixed = gather(step, weights[parity * UNROLL + u], fades[parity * UNROLL + u], mixed)
            for u in range(UNROLL):
                step = jnp.maximum((trip - 1) * UNROLL + u, 0)
                slot = (1 - parity) * UNROLL + u
                top, fade = weigh(step, scores[slot], weights[slot], top)
                fades = fades[:slot] + (fade,) + fades[slot + 1 :]
            for u in range(UNROLL):
                score(trip * UNROLL + u, scores[parity * UNROLL + u])
        return top, mixed, fades

    row = jnp.zeros((1, TILE), f32)
    ones = jnp.ones((16, GROUP * TILE), bf16)
    for slot in range(UNROLL, 2 * UNROLL):
        scores[slot][...] = jnp.zeros_like(scores[slot])
    for ref in weights:
        ref[...] = jnp.zeros_like(ref)
    pairs = lax.div(total_steps + 4 * UNROLL - 1, 2 * UNROLL)
    lax.fori_loop(0, pairs, body, (row, jnp.zeros((HD + 16, TILE), f32), (row,) * (2 * UNROLL)))


def attend(steps, slope, q, prior, own, later):
    smem = pl.BlockSpec(memory_space=pltpu.SMEM)
    vmem = pl.BlockSpec(memory_space=pltpu.VMEM)
    anywhere = pl.BlockSpec(memory_space=pl.ANY)
    return pl.pallas_call(
        attend_kernel,
        out_shape=jax.ShapeDtypeStruct((TB, HD, TILE), bf16),
        in_specs=[smem, smem, vmem, anywhere, anywhere, anywhere],
        out_specs=vmem,
        scratch_shapes=[
            pltpu.VMEM((3 * TB, 2 * HD, TILE), bf16),
            pltpu.SemaphoreType.DMA((3,)),
        ]
        + [pltpu.VMEM((GROUP * HD, 2 * TILE), f32)] * (2 * UNROLL)
        + [pltpu.VMEM((GROUP * TILE, TILE), bf16)] * (2 * UNROLL),
        compiler_params=pltpu.CompilerParams(vmem_limit_bytes=12 * 2**20),
        name="attend",
    )(steps, slope, q, prior, own, later)


def exchange(array):
    return lax.all_to_all(array, "head", split_axis=0, concat_axis=0, tiled=True)


def per_device(queries, keys, values, slopes, layer, mask, perm):
    block = lax.axis_index("blk").astype(i32).reshape(1)
    place = lax.axis_index("head").astype(i32).reshape(1)
    swap = jnp.where(block < lax.axis_size("blk") // 2, 0, 2)
    head = jnp.where(place % 2 == 0, place, place ^ swap)
    slope = lax.dynamic_slice_in_dim(slopes, head[0], 1)
    own = exchange(pack_kv(swap, keys, values))
    packed = pack_q(swap, queries)
    steps = table(block, perm, layer, mask)
    own, packed, steps, slope = lax.optimization_barrier((own, packed, steps, slope))
    prior = from_behind(own, 1)
    later = from_behind(own, -1)
    q = exchange(packed)
    mixed = attend(steps, slope, q, prior, own, later)
    return unpack(swap, exchange(mixed))


def solution(mesh):
    rows = P(("blk", "head"), None)
    return jax.shard_map(
        per_device,
        mesh=mesh,
        in_specs=(rows, rows, rows, P(), P(), P(), P()),
        out_specs=rows,
        check_vma=False,
    )
```

```python
import math

import jax
import jax.numpy as jnp
from jax import lax
from jax.experimental import pallas as pl
from jax.experimental.pallas import tpu as pltpu
from jax.sharding import PartitionSpec as P

HD = 64
HEADS = 32
TILE = 128
TB = 32
TILES = 256
KCAP = 9
GROUP = 3
UNROLL = 3
PARTS = 2
MOST_STEPS = 256
LOWEST = -1e30
EXPONENT = math.log2(math.e)

f32 = jnp.float32
bf16 = jnp.bfloat16
i32 = jnp.int32


def place_of(head, swap):
    if head % 2 == 0:
        return head
    return head - swap if head & 2 else head + swap


def swapped(value, odd):
    blocks, heads = lax.axis_size("blk"), lax.axis_size("head")
    pairs = []
    for block in range(blocks):
        target = (block + (1 if block % 2 == odd else -1)) % blocks
        crosses = 2 * block // blocks != 2 * target // blocks
        for place in range(heads):
            other = place ^ 2 if crosses and place % 2 else place
            pairs.append((block * heads + place, target * heads + other))
    return lax.ppermute(value, ("blk", "head"), pairs)


def pack_kv_kernel(swap_ref, k_hbm, v_hbm, kv_hbm, k_ref, v_ref, kv_ref, k_sem, v_sem, kv_sem):
    width = HEADS * HD // PARTS
    heads = HEADS // PARTS
    loads, stores = [], []
    for part in range(PARTS):
        columns = pl.ds(part * width, width)
        k_load = pltpu.make_async_copy(k_hbm.at[:, columns], k_ref.at[part], k_sem.at[part])
        v_load = pltpu.make_async_copy(v_hbm.at[:, columns], v_ref.at[part], v_sem.at[part])
        k_load.start()
        v_load.start()
        loads.append((k_load, v_load))
    for part in range(PARTS):
        loads[part][0].wait()
        loads[part][1].wait()
        for pair in range(heads // 2):
            columns = slice(pair * 128, pair * 128 + 128)
            one = part * heads + 2 * pair
            two = place_of(one + 1, swap_ref[0])
            k = k_ref[part, :, columns]
            upper, lower = k[:64], k[64:]
            kv_ref[one, :64, :] = jnp.concatenate([upper[:, :64], lower[:, :64]], axis=1)
            kv_ref[two, :64, :] = jnp.concatenate([upper[:, 64:], lower[:, 64:]], axis=1)
            v = v_ref[part, :, columns].T
            kv_ref[one, 64:, :] = v[:64]
            kv_ref[two, 64:, :] = v[64:]
        chunk = pl.ds(part * heads, heads)
        store = pltpu.make_async_copy(kv_ref.at[chunk], kv_hbm.at[chunk], kv_sem.at[part])
        store.start()
        stores.append(store)
    for store in stores:
        store.wait()


def pack_kv(swap, keys, values):
    anywhere = pl.BlockSpec(memory_space=pl.ANY)
    return pl.pallas_call(
        pack_kv_kernel,
        out_shape=jax.ShapeDtypeStruct((HEADS, 128, 128), bf16),
        in_specs=[pl.BlockSpec(memory_space=pltpu.SMEM)] + [anywhere] * 2,
        out_specs=anywhere,
        scratch_shapes=[pltpu.VMEM((PARTS, 128, HEADS * HD // PARTS), bf16)] * 2
        + [pltpu.VMEM((HEADS, 128, 128), bf16)]
        + [pltpu.SemaphoreType.DMA((PARTS,))] * 3,
        name="pack_kv",
    )(swap, keys, values)


def pack_q_kernel(swap_ref, q_ref, out_ref):
    for pair in range(HEADS // 2):
        q = q_ref[:, pair * 128 : pair * 128 + 128].T
        out_ref[2 * pair] = q[:64]
        out_ref[place_of(2 * pair + 1, swap_ref[0])] = q[64:]


def pack_q(swap, queries):
    return pl.pallas_call(
        pack_q_kernel,
        out_shape=jax.ShapeDtypeStruct((HEADS, HD, 128), bf16),
        in_specs=[pl.BlockSpec(memory_space=pltpu.SMEM), pl.BlockSpec(memory_space=pltpu.VMEM)],
        out_specs=pl.BlockSpec(memory_space=pltpu.VMEM),
        name="pack_q",
    )(swap, queries)


def unpack_kernel(swap_ref, in_ref, out_ref):
    for pair in range(HEADS // 2):
        two = place_of(2 * pair + 1, swap_ref[0])
        both = jnp.concatenate([in_ref[2 * pair], in_ref[two]], axis=0)
        out_ref[:, pair * 128 : pair * 128 + 128] = both.T


def unpack(swap, array):
    return pl.pallas_call(
        unpack_kernel,
        out_shape=jax.ShapeDtypeStruct((128, HEADS * HD), bf16),
        in_specs=[pl.BlockSpec(memory_space=pltpu.SMEM), pl.BlockSpec(memory_space=pltpu.VMEM)],
        out_specs=pl.BlockSpec(memory_space=pltpu.VMEM),
        compiler_params=pltpu.CompilerParams(vmem_limit_bytes=8 * 2**20),
        name="unpack",
    )(swap, array)


def iota(shape, dim):
    return lax.broadcasted_iota(i32, shape, dim)


def exact_dot(a, b):
    return jnp.dot(a.astype(bf16), b.astype(bf16), preferred_element_type=f32)


def table_kernel(block_ref, perm_ref, layer_ref, mask_ref, out_ref):
    block = block_ref[0]
    shift = lax.rem(TILES + TB - block * TB, TILES)
    perm = pltpu.roll(jnp.broadcast_to(perm_ref[...], (8, TILES)), shift, 1)[:1, :128]
    select = (perm == iota((TILES, 128), 0)).astype(f32)
    select_t = select.T
    own_select = select_t[TB : 2 * TB]
    columns = exact_dot(mask_ref[...].astype(f32), select)
    allowed = exact_dot(own_select, columns)
    allowed = jnp.where(iota((TB, 128), 1) < 3 * TB, allowed, 0.0)
    layer = layer_ref[...].astype(f32)
    layer_row = exact_dot(jnp.broadcast_to(layer, (8, TILES)), select)[:1]
    layer_own = jnp.sum(own_select * layer, axis=1, keepdims=True)
    gap = jnp.abs(layer_own - layer_row)
    before = (iota((128, 128), 0) < iota((128, 128), 1)).astype(f32)
    place = exact_dot(allowed, before)
    place = jnp.where(allowed > 0.5, place, 200.0)
    count = jnp.sum(allowed, axis=1, keepdims=True)
    steps = jnp.zeros((TB, 1), f32)
    for filled in range(0, 3 * KCAP, GROUP):
        steps = steps + (count > filled + 0.5).astype(f32)
    steps = jnp.broadcast_to(steps, (TB, 128))
    earlier = (iota((TB, TB), 1) < iota((TB, TB), 0)).astype(f32)
    start = exact_dot(earlier, steps)
    start = jnp.concatenate([start, start], axis=1)
    steps = jnp.concatenate([steps, steps], axis=1)
    now = iota((TB, MOST_STEPS), 1).astype(f32)
    hit = ((start <= now) & (now < start + steps)).astype(f32)
    covered = jnp.sum(hit, axis=0, keepdims=True)
    own_tile = jnp.sum(hit * iota((TB, MOST_STEPS), 0).astype(f32), axis=0, keepdims=True)
    own_tile = jnp.where(covered > 0.5, own_tile, TB - 1.0)
    within = jnp.sum(hit * (now - start), axis=0, keepdims=True)
    opening = (covered > 0.5) & (within < 0.5)
    total = jnp.sum(steps, axis=0, keepdims=True)
    place_t = exact_dot(place.T, hit)
    gap_t = exact_dot(gap.T, hit)
    tile = iota((128, MOST_STEPS), 0).astype(f32)
    rows = [own_tile, opening.astype(f32), total]
    gaps = []
    for g in range(GROUP):
        chosen = ((place_t == within * GROUP + g) & (covered > 0.5)).astype(f32)
        present = jnp.sum(chosen, axis=0, keepdims=True)
        rows.append(jnp.sum(chosen * tile, axis=0, keepdims=True))
        gaps.append(jnp.where(present > 0.5, jnp.sum(chosen * gap_t, axis=0, keepdims=True), -1.0))
    rows = rows + gaps
    rows = rows + [jnp.zeros((1, MOST_STEPS), f32)] * (16 - len(rows))
    out_ref[...] = jnp.concatenate(rows, axis=0).astype(i32)


def table(block, perm, layer, mask):
    return pl.pallas_call(
        table_kernel,
        out_shape=jax.ShapeDtypeStruct((16, MOST_STEPS), i32),
        in_specs=[pl.BlockSpec(memory_space=pltpu.SMEM)] + [pl.BlockSpec(memory_space=pltpu.VMEM)] * 3,
        out_specs=pl.BlockSpec(memory_space=pltpu.VMEM),
        name="table",
    )(block, perm.reshape(1, TILES), layer.reshape(1, TILES), mask)


def attend_kernel(
    table_ref,
    slope_ref,
    block_ref,
    q_ref,
    first_ref,
    own_ref,
    second_ref,
    out_ref,
    kv,
    arrived,
    *buffers,
):
    scores, weights = buffers[: 2 * UNROLL], buffers[2 * UNROLL :]
    side = pl.multiple_of(lax.rem(block_ref[0], 2) * (2 * TB), TB)
    copies = [
        pltpu.make_async_copy(source, kv.at[pl.ds(place, TB)], arrived.at[index])
        for index, (source, place) in enumerate(
            ((first_ref, side), (own_ref, TB), (second_ref, 2 * TB - side))
        )
    ]
    for copy in copies:
        copy.start()
    scale = EXPONENT / math.sqrt(HD)
    slope = slope_ref[0] * EXPONENT
    total_steps = table_ref[2, 0]
    zeros = jnp.zeros((HD, TILE), bf16)
    for copy in copies:
        copy.wait()

    def score(step, into):
        q = q_ref[table_ref[0, step]]
        q = jnp.concatenate(
            [jnp.concatenate([q, zeros], axis=1), jnp.concatenate([zeros, q], axis=1)], axis=0
        )
        k = jnp.concatenate([kv[table_ref[3 + g, step], :HD, :] for g in range(GROUP)], axis=0)
        into[...] = jnp.dot(k, q, preferred_element_type=f32)

    def weigh(step, source, into, top):
        first = table_ref[1, step] == 1
        biases = []
        top = jnp.where(first, LOWEST, top)
        new_top = top
        for g in range(GROUP):
            gap = table_ref[3 + GROUP + g, step]
            biases.append(jnp.where(gap < 0, -LOWEST, slope * gap.astype(f32)))
            s = source[g * HD : g * HD + HD, :]
            s = jnp.maximum(s[:, :TILE], s[:, TILE:])
            s = jnp.max(s, axis=0, keepdims=True) * scale - biases[g]
            new_top = jnp.maximum(new_top, s)
        for g in range(GROUP):
            s = source[g * HD : g * HD + HD, :]
            offset = new_top + biases[g]
            for half in range(2):
                w = jnp.exp2(s[:, half * TILE : half * TILE + TILE] * scale - offset)
                row = g * TILE + half * HD
                into[row : row + HD, :] = w.astype(bf16)
        return new_top, jnp.where(first, 0.0, jnp.exp2(top - new_top))

    def gather(step, source, fade, mixed):
        v = jnp.concatenate([kv[table_ref[3 + g, step], HD:, :] for g in range(GROUP)], axis=1)
        v = jnp.concatenate([v, ones], axis=0)
        mixed = mixed * fade + jnp.dot(v, source[...], preferred_element_type=f32)
        out_ref[table_ref[0, step]] = (mixed[:HD] * (1.0 / mixed[HD : HD + 1])).astype(bf16)
        return mixed

    def body(pair, carry):
        top, mixed, fades = carry
        for parity in range(2):
            trip = pair * 2 + parity
            for u in range(UNROLL):
                step = jnp.maximum((trip - 2) * UNROLL + u, 0)
                mixed = gather(step, weights[parity * UNROLL + u], fades[parity * UNROLL + u], mixed)
            for u in range(UNROLL):
                step = jnp.maximum((trip - 1) * UNROLL + u, 0)
                slot = (1 - parity) * UNROLL + u
                top, fade = weigh(step, scores[slot], weights[slot], top)
                fades = fades[:slot] + (fade,) + fades[slot + 1 :]
            for u in range(UNROLL):
                score(trip * UNROLL + u, scores[parity * UNROLL + u])
        return top, mixed, fades

    row = jnp.zeros((1, TILE), f32)
    ones = jnp.ones((16, GROUP * TILE), bf16)
    for slot in range(UNROLL, 2 * UNROLL):
        scores[slot][...] = jnp.zeros_like(scores[slot])
    for ref in weights:
        ref[...] = jnp.zeros_like(ref)
    pairs = lax.div(total_steps + 4 * UNROLL - 1, 2 * UNROLL)
    lax.fori_loop(0, pairs, body, (row, jnp.zeros((HD + 16, TILE), f32), (row,) * (2 * UNROLL)))


def attend(steps, slope, block, q, first, own, second):
    smem = pl.BlockSpec(memory_space=pltpu.SMEM)
    vmem = pl.BlockSpec(memory_space=pltpu.VMEM)
    anywhere = pl.BlockSpec(memory_space=pl.ANY)
    return pl.pallas_call(
        attend_kernel,
        out_shape=jax.ShapeDtypeStruct((TB, HD, TILE), bf16),
        in_specs=[smem, smem, smem, vmem, anywhere, anywhere, anywhere],
        out_specs=vmem,
        scratch_shapes=[
            pltpu.VMEM((3 * TB, 2 * HD, TILE), bf16),
            pltpu.SemaphoreType.DMA((3,)),
        ]
        + [pltpu.VMEM((GROUP * HD, 2 * TILE), f32)] * (2 * UNROLL)
        + [pltpu.VMEM((GROUP * TILE, TILE), bf16)] * (2 * UNROLL),
        compiler_params=pltpu.CompilerParams(vmem_limit_bytes=12 * 2**20),
        name="attend",
    )(steps, slope, block, q, first, own, second)


def exchange(array):
    return lax.all_to_all(array, "head", split_axis=0, concat_axis=0, tiled=True)


def per_device(queries, keys, values, slopes, layer, mask, perm):
    block = lax.axis_index("blk").astype(i32).reshape(1)
    place = lax.axis_index("head").astype(i32).reshape(1)
    swap = jnp.where(block < lax.axis_size("blk") // 2, 0, 2)
    head = jnp.where(place % 2 == 0, place, place ^ swap)
    slope = lax.dynamic_slice_in_dim(slopes, head[0], 1)
    own = exchange(pack_kv(swap, keys, values))
    packed = pack_q(swap, queries)
    steps = table(block, perm, layer, mask)
    own, packed, steps, slope = lax.optimization_barrier((own, packed, steps, slope))
    first = swapped(own, 1)
    second = swapped(own, 0)
    q = exchange(packed)
    mixed = attend(steps, slope, block, q, first, own, second)
    return unpack(swap, exchange(mixed))


def solution(mesh):
    rows = P(("blk", "head"), None)
    return jax.shard_map(
        per_device,
        mesh=mesh,
        in_specs=(rows, rows, rows, P(), P(), P(), P()),
        out_specs=rows,
        check_vma=False,
    )
```

```python
import math

import jax
import jax.numpy as jnp
from jax import lax
from jax.experimental import pallas as pl
from jax.experimental.pallas import tpu as pltpu
from jax.sharding import PartitionSpec as P

HD = 64
HEADS = 32
TILE = 128
TB = 32
TILES = 256
KCAP = 9
GROUP = 3
UNROLL = 16
PARTS = 2
MOST_STEPS = 256
LOWEST = -1e30
EXPONENT = math.log2(math.e)

f32 = jnp.float32
bf16 = jnp.bfloat16
i32 = jnp.int32


def place_of(head, swap):
    if head % 2 == 0:
        return head
    return head - swap if head & 2 else head + swap


def swapped(value, odd):
    blocks, heads = lax.axis_size("blk"), lax.axis_size("head")
    pairs = []
    for block in range(blocks):
        target = (block + (1 if block % 2 == odd else -1)) % blocks
        crosses = 2 * block // blocks != 2 * target // blocks
        for place in range(heads):
            other = place ^ 2 if crosses and place % 2 else place
            pairs.append((block * heads + place, target * heads + other))
    return lax.ppermute(value, ("blk", "head"), pairs)


def pack_kv_kernel(swap_ref, k_hbm, v_hbm, kv_hbm, k_ref, v_ref, kv_ref, k_sem, v_sem, kv_sem):
    width = HEADS * HD // PARTS
    heads = HEADS // PARTS
    loads, stores = [], []
    for part in range(PARTS):
        columns = pl.ds(part * width, width)
        k_load = pltpu.make_async_copy(k_hbm.at[:, columns], k_ref.at[part], k_sem.at[part])
        v_load = pltpu.make_async_copy(v_hbm.at[:, columns], v_ref.at[part], v_sem.at[part])
        k_load.start()
        v_load.start()
        loads.append((k_load, v_load))
    for part in range(PARTS):
        loads[part][0].wait()
        loads[part][1].wait()
        for pair in range(heads // 2):
            columns = slice(pair * 128, pair * 128 + 128)
            one = part * heads + 2 * pair
            two = place_of(one + 1, swap_ref[0])
            k = k_ref[part, :, columns]
            upper, lower = k[:64], k[64:]
            kv_ref[one, :64, :] = jnp.concatenate([upper[:, :64], lower[:, :64]], axis=1)
            kv_ref[two, :64, :] = jnp.concatenate([upper[:, 64:], lower[:, 64:]], axis=1)
            v = v_ref[part, :, columns].T
            kv_ref[one, 64:, :] = v[:64]
            kv_ref[two, 64:, :] = v[64:]
        chunk = pl.ds(part * heads, heads)
        store = pltpu.make_async_copy(kv_ref.at[chunk], kv_hbm.at[chunk], kv_sem.at[part])
        store.start()
        stores.append(store)
    for store in stores:
        store.wait()


def pack_kv(swap, keys, values):
    anywhere = pl.BlockSpec(memory_space=pl.ANY)
    return pl.pallas_call(
        pack_kv_kernel,
        out_shape=jax.ShapeDtypeStruct((HEADS, 128, 128), bf16),
        in_specs=[pl.BlockSpec(memory_space=pltpu.SMEM)] + [anywhere] * 2,
        out_specs=anywhere,
        scratch_shapes=[pltpu.VMEM((PARTS, 128, HEADS * HD // PARTS), bf16)] * 2
        + [pltpu.VMEM((HEADS, 128, 128), bf16)]
        + [pltpu.SemaphoreType.DMA((PARTS,))] * 3,
        name="pack_kv",
    )(swap, keys, values)


def pack_q_kernel(swap_ref, q_ref, out_ref):
    for pair in range(HEADS // 2):
        q = q_ref[:, pair * 128 : pair * 128 + 128].T
        out_ref[2 * pair] = q[:64]
        out_ref[place_of(2 * pair + 1, swap_ref[0])] = q[64:]


def pack_q(swap, queries):
    return pl.pallas_call(
        pack_q_kernel,
        out_shape=jax.ShapeDtypeStruct((HEADS, HD, 128), bf16),
        in_specs=[pl.BlockSpec(memory_space=pltpu.SMEM), pl.BlockSpec(memory_space=pltpu.VMEM)],
        out_specs=pl.BlockSpec(memory_space=pltpu.VMEM),
        name="pack_q",
    )(swap, queries)


def unpack_kernel(swap_ref, in_ref, out_ref):
    for pair in range(HEADS // 2):
        two = place_of(2 * pair + 1, swap_ref[0])
        both = jnp.concatenate([in_ref[2 * pair], in_ref[two]], axis=0)
        out_ref[:, pair * 128 : pair * 128 + 128] = both.T


def unpack(swap, array):
    return pl.pallas_call(
        unpack_kernel,
        out_shape=jax.ShapeDtypeStruct((128, HEADS * HD), bf16),
        in_specs=[pl.BlockSpec(memory_space=pltpu.SMEM), pl.BlockSpec(memory_space=pltpu.VMEM)],
        out_specs=pl.BlockSpec(memory_space=pltpu.VMEM),
        compiler_params=pltpu.CompilerParams(vmem_limit_bytes=8 * 2**20),
        name="unpack",
    )(swap, array)


def iota(shape, dim):
    return lax.broadcasted_iota(i32, shape, dim)


def exact_dot(a, b):
    return jnp.dot(a.astype(bf16), b.astype(bf16), preferred_element_type=f32)


def table_kernel(block_ref, perm_ref, layer_ref, mask_ref, out_ref):
    block = block_ref[0]
    shift = lax.rem(TILES + TB - block * TB, TILES)
    perm = pltpu.roll(jnp.broadcast_to(perm_ref[...], (8, TILES)), shift, 1)[:1, :128]
    select = (perm == iota((TILES, 128), 0)).astype(f32)
    select_t = select.T
    own_select = select_t[TB : 2 * TB]
    columns = exact_dot(mask_ref[...].astype(f32), select)
    allowed = exact_dot(own_select, columns)
    allowed = jnp.where(iota((TB, 128), 1) < 3 * TB, allowed, 0.0)
    layer = layer_ref[...].astype(f32)
    layer_row = exact_dot(jnp.broadcast_to(layer, (8, TILES)), select)[:1]
    layer_own = jnp.sum(own_select * layer, axis=1, keepdims=True)
    gap = jnp.abs(layer_own - layer_row)
    before = (iota((128, 128), 0) < iota((128, 128), 1)).astype(f32)
    place = exact_dot(allowed, before)
    place = jnp.where(allowed > 0.5, place, 200.0)
    count = jnp.sum(allowed, axis=1, keepdims=True)
    steps = jnp.zeros((TB, 1), f32)
    for filled in range(0, 3 * KCAP, GROUP):
        steps = steps + (count > filled + 0.5).astype(f32)
    steps = jnp.broadcast_to(steps, (TB, 128))
    earlier = (iota((TB, TB), 1) < iota((TB, TB), 0)).astype(f32)
    start = exact_dot(earlier, steps)
    start = jnp.concatenate([start, start], axis=1)
    steps = jnp.concatenate([steps, steps], axis=1)
    now = iota((TB, MOST_STEPS), 1).astype(f32)
    hit = ((start <= now) & (now < start + steps)).astype(f32)
    covered = jnp.sum(hit, axis=0, keepdims=True)
    own_tile = jnp.sum(hit * iota((TB, MOST_STEPS), 0).astype(f32), axis=0, keepdims=True)
    own_tile = jnp.where(covered > 0.5, own_tile, TB - 1.0)
    within = jnp.sum(hit * (now - start), axis=0, keepdims=True)
    opening = (covered > 0.5) & (within < 0.5)
    total = jnp.sum(steps, axis=0, keepdims=True)
    place_t = exact_dot(place.T, hit)
    gap_t = exact_dot(gap.T, hit)
    tile = iota((128, MOST_STEPS), 0).astype(f32)
    rows = [own_tile, opening.astype(f32), total]
    gaps = []
    for g in range(GROUP):
        chosen = ((place_t == within * GROUP + g) & (covered > 0.5)).astype(f32)
        present = jnp.sum(chosen, axis=0, keepdims=True)
        rows.append(jnp.sum(chosen * tile, axis=0, keepdims=True))
        gaps.append(jnp.where(present > 0.5, jnp.sum(chosen * gap_t, axis=0, keepdims=True), -1.0))
    rows = rows + gaps
    rows = rows + [jnp.zeros((1, MOST_STEPS), f32)] * (16 - len(rows))
    out_ref[...] = jnp.concatenate(rows, axis=0).astype(i32)


def table(block, perm, layer, mask):
    return pl.pallas_call(
        table_kernel,
        out_shape=jax.ShapeDtypeStruct((16, MOST_STEPS), i32),
        in_specs=[pl.BlockSpec(memory_space=pltpu.SMEM)] + [pl.BlockSpec(memory_space=pltpu.VMEM)] * 3,
        out_specs=pl.BlockSpec(memory_space=pltpu.VMEM),
        name="table",
    )(block, perm.reshape(1, TILES), layer.reshape(1, TILES), mask)


def attend_kernel(
    table_ref,
    slope_ref,
    block_ref,
    q_ref,
    first_ref,
    own_ref,
    second_ref,
    out_ref,
    kv,
    arrived,
    *buffers,
):
    scores, weights = buffers[:UNROLL], buffers[UNROLL:]
    side = pl.multiple_of(lax.rem(block_ref[0], 2) * (2 * TB), TB)
    copies = [
        pltpu.make_async_copy(source, kv.at[pl.ds(place, TB)], arrived.at[index])
        for index, (source, place) in enumerate(
            ((first_ref, side), (own_ref, TB), (second_ref, 2 * TB - side))
        )
    ]
    for copy in copies:
        copy.start()
    scale = EXPONENT / math.sqrt(HD)
    slope = slope_ref[0] * EXPONENT
    total_steps = table_ref[2, 0]
    zeros = jnp.zeros((HD, TILE), bf16)
    for copy in copies:
        copy.wait()

    def score(step, into):
        q = q_ref[table_ref[0, step]]
        q = jnp.concatenate(
            [jnp.concatenate([q, zeros], axis=1), jnp.concatenate([zeros, q], axis=1)], axis=0
        )
        k = jnp.concatenate([kv[table_ref[3 + g, step], :HD, :] for g in range(GROUP)], axis=0)
        s = jnp.dot(k, q, preferred_element_type=f32)
        into[...] = s
        s = jnp.maximum(s[:, :TILE], s[:, TILE:])
        return tuple(s[g * HD : g * HD + HD].reshape(8, 8, TILE).max(axis=0) for g in range(GROUP))

    def weigh(step, source, peaks, into, top):
        first = table_ref[1, step] == 1
        biases = []
        top = jnp.where(first, LOWEST, top)
        highest = None
        for g in range(GROUP):
            gap = table_ref[3 + GROUP + g, step]
            biases.append(jnp.where(gap < 0, -LOWEST, slope * gap.astype(f32)))
            s = peaks[g] * scale - biases[g]
            highest = s if highest is None else jnp.maximum(highest, s)
        new_top = jnp.maximum(top, jnp.max(highest, axis=0, keepdims=True))
        for g in range(GROUP):
            s = source[g * HD : g * HD + HD, :]
            offset = new_top + biases[g]
            for half in range(2):
                w = jnp.exp2(s[:, half * TILE : half * TILE + TILE] * scale - offset)
                row = g * TILE + half * HD
                into[row : row + HD, :] = w.astype(bf16)
        return new_top, jnp.where(first, 0.0, jnp.exp2(top - new_top))

    def gather(step, source, fade, mixed):
        v = jnp.concatenate([kv[table_ref[3 + g, step], HD:, :] for g in range(GROUP)], axis=1)
        v = jnp.concatenate([v, ones], axis=0)
        mixed = mixed * fade + jnp.dot(v, source[...], preferred_element_type=f32)
        out_ref[table_ref[0, step]] = (mixed[:HD] * (1.0 / mixed[HD : HD + 1])).astype(bf16)
        return mixed

    def body(trip, carry):
        top, mixed, fades, peaks = carry
        new_fades, new_peaks = [], []
        for u in range(UNROLL):
            mixed = gather((trip - 2) * UNROLL + u, weights[u], fades[u], mixed)
            top, fade = weigh((trip - 1) * UNROLL + u, scores[u], peaks[u], weights[u], top)
            new_fades.append(fade)
            new_peaks.append(score(trip * UNROLL + u, scores[u]))
        return top, mixed, tuple(new_fades), tuple(new_peaks)

    ones = jnp.ones((16, GROUP * TILE), bf16)
    trips = lax.div(total_steps + UNROLL - 1, UNROLL)
    top = q_ref[0, :1, :].astype(f32)
    mixed = jnp.zeros((HD + 16, TILE), f32)
    peaks = [score(u, scores[u]) for u in range(UNROLL)]
    fades = [None] * UNROLL
    for u in range(UNROLL):
        top, fades[u] = weigh(u, scores[u], peaks[u], weights[u], top)
        peaks[u] = score(UNROLL + u, scores[u])
    carry = (top, mixed, tuple(fades), tuple(peaks))
    top, mixed, fades, peaks = lax.fori_loop(2, trips, body, carry)
    late = []
    for u in range(UNROLL):
        mixed = gather((trips - 2) * UNROLL + u, weights[u], fades[u], mixed)
        top, fade = weigh((trips - 1) * UNROLL + u, scores[u], peaks[u], weights[u], top)
        late.append(fade)
    for u in range(UNROLL):
        mixed = gather((trips - 1) * UNROLL + u, weights[u], late[u], mixed)


def attend(steps, slope, block, q, first, own, second):
    smem = pl.BlockSpec(memory_space=pltpu.SMEM)
    vmem = pl.BlockSpec(memory_space=pltpu.VMEM)
    anywhere = pl.BlockSpec(memory_space=pl.ANY)
    return pl.pallas_call(
        attend_kernel,
        out_shape=jax.ShapeDtypeStruct((TB, HD, TILE), bf16),
        in_specs=[smem, smem, smem, vmem, anywhere, anywhere, anywhere],
        out_specs=vmem,
        scratch_shapes=[
            pltpu.VMEM((3 * TB, 2 * HD, TILE), bf16),
            pltpu.SemaphoreType.DMA((3,)),
        ]
        + [pltpu.VMEM((GROUP * HD, 2 * TILE), f32)] * UNROLL
        + [pltpu.VMEM((GROUP * TILE, TILE), bf16)] * UNROLL,
        compiler_params=pltpu.CompilerParams(vmem_limit_bytes=12 * 2**20),
        name="attend",
    )(steps, slope, block, q, first, own, second)


def exchange(array):
    return lax.all_to_all(array, "head", split_axis=0, concat_axis=0, tiled=True)


def per_device(queries, keys, values, slopes, layer, mask, perm):
    block = lax.axis_index("blk").astype(i32).reshape(1)
    place = lax.axis_index("head").astype(i32).reshape(1)
    swap = jnp.where(block < lax.axis_size("blk") // 2, 0, 2)
    head = jnp.where(place % 2 == 0, place, place ^ swap)
    slope = lax.dynamic_slice_in_dim(slopes, head[0], 1)
    own = exchange(pack_kv(swap, keys, values))
    packed = pack_q(swap, queries)
    steps = table(block, perm, layer, mask)
    own, packed, steps, slope = lax.optimization_barrier((own, packed, steps, slope))
    first = swapped(own, 1)
    second = swapped(own, 0)
    q = exchange(packed)
    mixed = attend(steps, slope, block, q, first, own, second)
    return unpack(swap, exchange(mixed))


def solution(mesh):
    rows = P(("blk", "head"), None)
    return jax.shard_map(
        per_device,
        mesh=mesh,
        in_specs=(rows, rows, rows, P(), P(), P(), P()),
        out_specs=rows,
        check_vma=False,
    )
```

```python
import math

import jax
import jax.numpy as jnp
from jax import lax
from jax.experimental import pallas as pl
from jax.experimental.pallas import tpu as pltpu
from jax.sharding import PartitionSpec as P

HD = 64
HEADS = 32
TILE = 128
TB = 32
TILES = 256
KCAP = 9
GROUP = 3
UNROLL = 16
PARTS = 2
MOST_STEPS = 256
LOWEST = -1e30
EXPONENT = math.log2(math.e)

f32 = jnp.float32
bf16 = jnp.bfloat16
i32 = jnp.int32


def place_of(head, swap):
    if head % 2 == 0:
        return head
    return head - swap if head & 2 else head + swap


def swapped(value, odd):
    blocks, heads = lax.axis_size("blk"), lax.axis_size("head")
    pairs = []
    for block in range(blocks):
        target = (block + (1 if block % 2 == odd else -1)) % blocks
        crosses = 2 * block // blocks != 2 * target // blocks
        for place in range(heads):
            other = place ^ 2 if crosses and place % 2 else place
            pairs.append((block * heads + place, target * heads + other))
    return lax.ppermute(value, ("blk", "head"), pairs)


def pack_kv_kernel(swap_ref, k_hbm, v_hbm, kv_hbm, k_ref, v_ref, kv_ref, k_sem, v_sem, kv_sem):
    width = HEADS * HD // PARTS
    heads = HEADS // PARTS
    loads, stores = [], []
    for part in range(PARTS):
        columns = pl.ds(part * width, width)
        k_load = pltpu.make_async_copy(k_hbm.at[:, columns], k_ref.at[part], k_sem.at[part])
        v_load = pltpu.make_async_copy(v_hbm.at[:, columns], v_ref.at[part], v_sem.at[part])
        k_load.start()
        v_load.start()
        loads.append((k_load, v_load))
    for part in range(PARTS):
        loads[part][0].wait()
        loads[part][1].wait()
        for pair in range(heads // 2):
            columns = slice(pair * 128, pair * 128 + 128)
            one = part * heads + 2 * pair
            two = place_of(one + 1, swap_ref[0])
            k = k_ref[part, :, columns]
            upper, lower = k[:64], k[64:]
            kv_ref[one, :64, :] = jnp.concatenate([upper[:, :64], lower[:, :64]], axis=1)
            kv_ref[two, :64, :] = jnp.concatenate([upper[:, 64:], lower[:, 64:]], axis=1)
            v = v_ref[part, :, columns].T
            kv_ref[one, 64:, :] = v[:64]
            kv_ref[two, 64:, :] = v[64:]
        chunk = pl.ds(part * heads, heads)
        store = pltpu.make_async_copy(kv_ref.at[chunk], kv_hbm.at[chunk], kv_sem.at[part])
        store.start()
        stores.append(store)
    for store in stores:
        store.wait()


def pack_kv(swap, keys, values):
    anywhere = pl.BlockSpec(memory_space=pl.ANY)
    return pl.pallas_call(
        pack_kv_kernel,
        out_shape=jax.ShapeDtypeStruct((HEADS, 128, 128), bf16),
        in_specs=[pl.BlockSpec(memory_space=pltpu.SMEM)] + [anywhere] * 2,
        out_specs=anywhere,
        scratch_shapes=[pltpu.VMEM((PARTS, 128, HEADS * HD // PARTS), bf16)] * 2
        + [pltpu.VMEM((HEADS, 128, 128), bf16)]
        + [pltpu.SemaphoreType.DMA((PARTS,))] * 3,
        name="pack_kv",
    )(swap, keys, values)


def pack_q_kernel(swap_ref, q_ref, out_ref):
    for pair in range(HEADS // 2):
        q = q_ref[:, pair * 128 : pair * 128 + 128].T
        out_ref[2 * pair] = q[:64]
        out_ref[place_of(2 * pair + 1, swap_ref[0])] = q[64:]


def pack_q(swap, queries):
    return pl.pallas_call(
        pack_q_kernel,
        out_shape=jax.ShapeDtypeStruct((HEADS, HD, 128), bf16),
        in_specs=[pl.BlockSpec(memory_space=pltpu.SMEM), pl.BlockSpec(memory_space=pltpu.VMEM)],
        out_specs=pl.BlockSpec(memory_space=pltpu.VMEM),
        name="pack_q",
    )(swap, queries)


def unpack_kernel(swap_ref, in_ref, out_ref):
    for pair in range(HEADS // 2):
        two = place_of(2 * pair + 1, swap_ref[0])
        both = jnp.concatenate([in_ref[2 * pair], in_ref[two]], axis=0)
        out_ref[:, pair * 128 : pair * 128 + 128] = both.T


def unpack(swap, array):
    return pl.pallas_call(
        unpack_kernel,
        out_shape=jax.ShapeDtypeStruct((128, HEADS * HD), bf16),
        in_specs=[pl.BlockSpec(memory_space=pltpu.SMEM), pl.BlockSpec(memory_space=pltpu.VMEM)],
        out_specs=pl.BlockSpec(memory_space=pltpu.VMEM),
        compiler_params=pltpu.CompilerParams(vmem_limit_bytes=8 * 2**20),
        name="unpack",
    )(swap, array)


def iota(shape, dim):
    return lax.broadcasted_iota(i32, shape, dim)


def exact_dot(a, b):
    return jnp.dot(a.astype(bf16), b.astype(bf16), preferred_element_type=f32)


def table_kernel(block_ref, perm_ref, layer_ref, mask_ref, out_ref):
    block = block_ref[0]
    shift = lax.rem(TILES + TB - block * TB, TILES)
    perm = pltpu.roll(jnp.broadcast_to(perm_ref[...], (8, TILES)), shift, 1)[:1, :128]
    select = (perm == iota((TILES, 128), 0)).astype(f32)
    select_t = select.T
    own_select = select_t[TB : 2 * TB]
    columns = exact_dot(mask_ref[...].astype(f32), select)
    allowed = exact_dot(own_select, columns)
    allowed = jnp.where(iota((TB, 128), 1) < 3 * TB, allowed, 0.0)
    layer = layer_ref[...].astype(f32)
    layer_row = exact_dot(jnp.broadcast_to(layer, (8, TILES)), select)[:1]
    layer_own = jnp.sum(own_select * layer, axis=1, keepdims=True)
    gap = jnp.abs(layer_own - layer_row)
    before = (iota((128, 128), 0) < iota((128, 128), 1)).astype(f32)
    place = exact_dot(allowed, before)
    place = jnp.where(allowed > 0.5, place, 200.0)
    count = jnp.sum(allowed, axis=1, keepdims=True)
    steps = jnp.zeros((TB, 1), f32)
    for filled in range(0, 3 * KCAP, GROUP):
        steps = steps + (count > filled + 0.5).astype(f32)
    steps = jnp.broadcast_to(steps, (TB, 128))
    earlier = (iota((TB, TB), 1) < iota((TB, TB), 0)).astype(f32)
    start = exact_dot(earlier, steps)
    start = jnp.concatenate([start, start], axis=1)
    steps = jnp.concatenate([steps, steps], axis=1)
    now = iota((TB, MOST_STEPS), 1).astype(f32)
    hit = ((start <= now) & (now < start + steps)).astype(f32)
    covered = jnp.sum(hit, axis=0, keepdims=True)
    own_tile = jnp.sum(hit * iota((TB, MOST_STEPS), 0).astype(f32), axis=0, keepdims=True)
    own_tile = jnp.where(covered > 0.5, own_tile, TB - 1.0)
    within = jnp.sum(hit * (now - start), axis=0, keepdims=True)
    opening = (covered > 0.5) & (within < 0.5)
    total = jnp.sum(steps, axis=0, keepdims=True)
    place_t = exact_dot(place.T, hit)
    gap_t = exact_dot(gap.T, hit)
    tile = iota((128, MOST_STEPS), 0).astype(f32)
    rows = [own_tile, opening.astype(f32), total]
    gaps = []
    for g in range(GROUP):
        chosen = ((place_t == within * GROUP + g) & (covered > 0.5)).astype(f32)
        present = jnp.sum(chosen, axis=0, keepdims=True)
        rows.append(jnp.sum(chosen * tile, axis=0, keepdims=True))
        gaps.append(jnp.where(present > 0.5, jnp.sum(chosen * gap_t, axis=0, keepdims=True), -1.0))
    rows[3:] = [other + 128.0 * (gap + 1.0) for other, gap in zip(rows[3:], gaps)]
    rows = rows + [jnp.zeros((1, MOST_STEPS), f32)] * (8 - len(rows))
    out_ref[...] = jnp.concatenate(rows, axis=0).astype(i32)


def table(block, perm, layer, mask):
    return pl.pallas_call(
        table_kernel,
        out_shape=jax.ShapeDtypeStruct((8, MOST_STEPS), i32),
        in_specs=[pl.BlockSpec(memory_space=pltpu.SMEM)] + [pl.BlockSpec(memory_space=pltpu.VMEM)] * 3,
        out_specs=pl.BlockSpec(memory_space=pltpu.VMEM),
        name="table",
    )(block, perm.reshape(1, TILES), layer.reshape(1, TILES), mask)


def attend_kernel(
    table_ref,
    slope_ref,
    block_ref,
    q_ref,
    first_ref,
    own_ref,
    second_ref,
    out_ref,
    kv,
    arrived,
    *buffers,
):
    scores, weights = buffers[:UNROLL], buffers[UNROLL:]
    side = pl.multiple_of(lax.rem(block_ref[0], 2) * (2 * TB), TB)
    copies = [
        pltpu.make_async_copy(source, kv.at[pl.ds(place, TB)], arrived.at[index])
        for index, (source, place) in enumerate(
            ((first_ref, side), (own_ref, TB), (second_ref, 2 * TB - side))
        )
    ]
    for copy in copies:
        copy.start()
    scale = EXPONENT / math.sqrt(HD)
    slope = slope_ref[0] * EXPONENT
    total_steps = table_ref[2, 0]
    zeros = jnp.zeros((HD, TILE), bf16)
    for copy in copies:
        copy.wait()

    def score(step, into):
        q = q_ref[table_ref[0, step]]
        q = jnp.concatenate(
            [jnp.concatenate([q, zeros], axis=1), jnp.concatenate([zeros, q], axis=1)], axis=0
        )
        k = jnp.concatenate([kv[table_ref[3 + g, step] & 127, :HD, :] for g in range(GROUP)], axis=0)
        s = jnp.dot(k, q, preferred_element_type=f32)
        into[...] = s
        s = jnp.maximum(s[:, :TILE], s[:, TILE:])
        return tuple(s[g * HD : g * HD + HD].reshape(8, 8, TILE).max(axis=0) for g in range(GROUP))

    def weigh(step, source, peaks, into, top):
        first = table_ref[1, step] == 1
        biases = []
        top = jnp.where(first, LOWEST, top)
        highest = None
        for g in range(GROUP):
            gap = (table_ref[3 + g, step] >> 7) - 1
            biases.append(jnp.where(gap < 0, -LOWEST, slope * gap.astype(f32)))
            s = peaks[g] * scale - biases[g]
            highest = s if highest is None else jnp.maximum(highest, s)
        new_top = jnp.maximum(top, jnp.max(highest, axis=0, keepdims=True))
        for g in range(GROUP):
            s = source[g * HD : g * HD + HD, :]
            offset = new_top + biases[g]
            for half in range(2):
                w = jnp.exp2(s[:, half * TILE : half * TILE + TILE] * scale - offset)
                row = g * TILE + half * HD
                into[row : row + HD, :] = w.astype(bf16)
        return new_top, jnp.where(first, 0.0, jnp.exp2(top - new_top))

    def gather(step, source, fade, mixed):
        v = jnp.concatenate([kv[table_ref[3 + g, step] & 127, HD:, :] for g in range(GROUP)], axis=1)
        v = jnp.concatenate([v, ones], axis=0)
        mixed = mixed * fade + jnp.dot(v, source[...], preferred_element_type=f32)
        out_ref[table_ref[0, step]] = (mixed[:HD] * (1.0 / mixed[HD : HD + 1])).astype(bf16)
        return mixed

    def body(trip, carry):
        top, mixed, fades, peaks = carry
        new_fades, new_peaks = [], []
        for u in range(UNROLL):
            mixed = gather((trip - 2) * UNROLL + u, weights[u], fades[u], mixed)
            top, fade = weigh((trip - 1) * UNROLL + u, scores[u], peaks[u], weights[u], top)
            new_fades.append(fade)
            new_peaks.append(score(trip * UNROLL + u, scores[u]))
        return top, mixed, tuple(new_fades), tuple(new_peaks)

    ones = jnp.ones((16, GROUP * TILE), bf16)
    trips = lax.div(total_steps + UNROLL - 1, UNROLL)
    top = q_ref[0, :1, :].astype(f32)
    mixed = jnp.zeros((HD + 16, TILE), f32)
    peaks = [score(u, scores[u]) for u in range(UNROLL)]
    fades = [None] * UNROLL
    for u in range(UNROLL):
        top, fades[u] = weigh(u, scores[u], peaks[u], weights[u], top)
        peaks[u] = score(UNROLL + u, scores[u])
    carry = (top, mixed, tuple(fades), tuple(peaks))
    top, mixed, fades, peaks = lax.fori_loop(2, trips, body, carry)
    late = []
    for u in range(UNROLL):
        mixed = gather((trips - 2) * UNROLL + u, weights[u], fades[u], mixed)
        top, fade = weigh((trips - 1) * UNROLL + u, scores[u], peaks[u], weights[u], top)
        late.append(fade)
    for u in range(UNROLL):
        mixed = gather((trips - 1) * UNROLL + u, weights[u], late[u], mixed)


def attend(steps, slope, block, q, first, own, second):
    smem = pl.BlockSpec(memory_space=pltpu.SMEM)
    vmem = pl.BlockSpec(memory_space=pltpu.VMEM)
    anywhere = pl.BlockSpec(memory_space=pl.ANY)
    return pl.pallas_call(
        attend_kernel,
        out_shape=jax.ShapeDtypeStruct((TB, HD, TILE), bf16),
        in_specs=[smem, smem, smem, vmem, anywhere, anywhere, anywhere],
        out_specs=vmem,
        scratch_shapes=[
            pltpu.VMEM((3 * TB, 2 * HD, TILE), bf16),
            pltpu.SemaphoreType.DMA((3,)),
        ]
        + [pltpu.VMEM((GROUP * HD, 2 * TILE), f32)] * UNROLL
        + [pltpu.VMEM((GROUP * TILE, TILE), bf16)] * UNROLL,
        compiler_params=pltpu.CompilerParams(vmem_limit_bytes=12 * 2**20),
        name="attend",
    )(steps, slope, block, q, first, own, second)


def exchange(array):
    return lax.all_to_all(array, "head", split_axis=0, concat_axis=0, tiled=True)


def per_device(queries, keys, values, slopes, layer, mask, perm):
    block = lax.axis_index("blk").astype(i32).reshape(1)
    place = lax.axis_index("head").astype(i32).reshape(1)
    swap = jnp.where(block < lax.axis_size("blk") // 2, 0, 2)
    head = jnp.where(place % 2 == 0, place, place ^ swap)
    slope = lax.dynamic_slice_in_dim(slopes, head[0], 1)
    own = exchange(pack_kv(swap, keys, values))
    packed = pack_q(swap, queries)
    steps = table(block, perm, layer, mask)
    own, packed, steps, slope = lax.optimization_barrier((own, packed, steps, slope))
    first = swapped(own, 1)
    second = swapped(own, 0)
    q = exchange(packed)
    mixed = attend(steps, slope, block, q, first, own, second)
    return unpack(swap, exchange(mixed))


def solution(mesh):
    rows = P(("blk", "head"), None)
    return jax.shard_map(
        per_device,
        mesh=mesh,
        in_specs=(rows, rows, rows, P(), P(), P(), P()),
        out_specs=rows,
        check_vma=False,
    )
```
